256 devices in a mesh: gx: 16 (over y, z_hi, core), gz: 4 (over x), ga: 4 (over z_lo).
Axes of the slice: x: 4, y: 4, z: 8 (z_hi: 2, z_lo: 4; z = z_hi * 4 + z_lo), core: 2. Of those that a mesh axis runs over, the one named last changes fastest.
Arguments:
- right_side: float32 [256, 128, 512], P('gx', 'ga', 'gz'), may hold values from -60 to 60, as said below
- diagonal: float32 [256, 128, 512], P('gx', 'ga', 'gz'), may hold values from 0.02 to 1
- element_features: bfloat16 [256, 32768], P(None, ('gx', 'gz', 'ga')), may hold values from -6 to 6
- sample_bank: bfloat16 [256, 1048576], P(None, ('gx', 'gz', 'ga')), may hold values from -6 to 6
- target_bank: bfloat16 [6, 1048576], P(None, ('gx', 'gz', 'ga')), may hold values from -6 to 6
- patch_index: int32 [524288], P(('gx', 'gz', 'ga')), may hold values from 0 to 4095
- w_first: bfloat16 [256, 256], replicated, may hold values from -0.375 to 0.375
- w_second: bfloat16 [256, 256], replicated, may hold values from -0.375 to 0.375
- w_third: bfloat16 [6, 256], replicated, may hold values from -0.375 to 0.375
Outputs:
- pressure: float32 [256, 128, 512], P('gx', 'ga', 'gz')
- residual: float32 [256, 128, 512], P('gx', 'ga', 'gz')
- step_first: float32 [256, 256], replicated
- step_second: float32 [256, 256], replicated
- step_third: float32 [6, 256], replicated
The draws below stay inside these ranges and needn't reach their ends.
Inputs may be any that keep to these rules, and one draw needn't show every extreme that they name: `right_side`: grows in magnitude along the first dimension. `patch_index`: each entry names a column of the sample_bank and target_bank block that lies on the same device as the entry.
All inputs are finite; a program needn't handle non-finite values.
Results may differ from the reference program's by a relative error of at most 0.0004.
The reference program's roundings to bfloat16 on the way count: a program that leaves them out, or rounds other values in their place, can miss the bound.
Values sent between devices are 32-bit elements; how exact they have to be, the bound alone decides.
No kernel may reach another device: no remote copies, remote signals or barrier semaphores. Data moves between devices by JAX's collectives and lax.ppermute only.
A program may use at most 64 MiB of HBM per device.

```python
import math
import jax
import jax.numpy as jnp
from jax import lax

CX = 16
CY = 32
CZ = 128
EL = 8
CH = 256
STRESS = 6
ITERS = 12
SAMPLES_DEV = 2048
BANK_DEV = 4096
NX = 256
NY = 128
NZ = 512
ELEMS = 32768
BANK = 1048576
SAMPLES = 524288
N_GX = 16
N_GZ = 4
N_GA = 4


def draw_right_side(key, part):
    position = jnp.arange(NX, dtype=jnp.float32) / NX
    growth = jnp.power(10.0, position)[:, None, None]
    random_part = jax.random.truncated_normal(key, -6.0, 6.0, (NX, NY, NZ), jnp.float32)
    return random_part * growth


def with_ends(result, key, low, high):
    longest = result.shape.index(max(result.shape))
    spots = []
    for shift in (0, 1):
        where = [jax.random.randint(jax.random.fold_in(key, axis), (), 0, length) for axis, length in enumerate(result.shape)]
        where[longest] = (where[longest] + shift) % result.shape[longest]
        spots.append(tuple(where))
    return result.at[spots[0]].set(low).at[spots[1]].set(high)


def level_of(own_key, dims, split, smallest, top_value):
    def one(axis_at, blocks):
        heights = jax.random.uniform(jax.random.fold_in(jax.random.fold_in(own_key, 6), axis_at), (blocks,), jnp.float32, smallest / len(split), top_value / len(split))
        return jnp.repeat(jnp.exp(heights), dims[axis_at] // blocks).reshape((-1,) + (1,) * (len(dims) - axis_at - 1))

    factor_of = one(*split[0])
    for cut in split[1:]:
        factor_of = factor_of * one(*cut)
    return factor_of


def scatter_about(rng, dims, scale, reach, cuts=(), kind=jnp.bfloat16):
    gain = level_of(rng, dims, cuts, -0.22, 0.18) if cuts else 1.0
    entries = jax.random.normal(rng, dims, jnp.float32) * scale * gain
    return jnp.minimum(jnp.maximum(entries, -reach), reach).astype(kind)


def setup_inputs(seed: int = 0) -> dict:
    arg_keys = jax.random.split(jax.random.key(seed), 10)
    return {
        "right_side": draw_right_side(jax.random.fold_in(arg_keys[9], 71), 0),
        "diagonal": jnp.clip(jnp.exp(math.log(1.0) - 3.912023 * jax.random.uniform(arg_keys[1], (NX, NY, NZ), jnp.float32) ** level_of(arg_keys[1], (NX, NY, NZ), ((0, 16), (1, 4), (2, 4)), -0.2, 0.2)), 0.02, 1.0),
        "element_features": scatter_about(arg_keys[2], (CH, ELEMS), 1.0, 6.0, ((1, 256),)),
        "sample_bank": scatter_about(arg_keys[3], (CH, BANK), 1.0, 6.0, ((1, 256),)),
        "target_bank": scatter_about(arg_keys[4], (STRESS, BANK), 1.0, 6.0, ((1, 256),)),
        "patch_index": with_ends(jax.random.randint(arg_keys[5], (SAMPLES,), 0, BANK_DEV), jax.random.fold_in(arg_keys[5], 1), 0, BANK_DEV - 1).astype(jnp.int32),
        "w_first": scatter_about(arg_keys[6], (CH, CH), CH ** -0.5, 0.375),
        "w_second": scatter_about(arg_keys[7], (CH, CH), CH ** -0.5, 0.375),
        "w_third": scatter_about(arg_keys[8], (STRESS, CH), CH ** -0.5, 0.375),
    }


taps = (1.6, -0.2, 8.0 / 315.0, -1.0 / 560.0)
center = 3.0 * 205.0 / 72.0
epsilon = 1e-06

def neighbours(padded):
    length_x = padded.shape[0] - 8
    length_y = padded.shape[1] - 8
    length_z = padded.shape[2] - 8
    summed = jnp.zeros((length_x, length_y, length_z), padded.dtype)
    for offset in range(1, 5):
        weight = taps[offset - 1]
        along_x = padded[4 + offset:4 + offset + length_x, 4:4 + length_y, 4:4 + length_z] + padded[4 - offset:4 - offset + length_x, 4:4 + length_y, 4:4 + length_z]
        along_y = padded[4:4 + length_x, 4 + offset:4 + offset + length_y, 4:4 + length_z] + padded[4:4 + length_x, 4 - offset:4 - offset + length_y, 4:4 + length_z]
        along_z = padded[4:4 + length_x, 4:4 + length_y, 4 + offset:4 + offset + length_z] + padded[4:4 + length_x, 4:4 + length_y, 4 - offset:4 - offset + length_z]
        summed = summed + weight * (along_x + along_y + along_z)
    return summed

def operate(padded, precond):
    return precond * padded[4:-4, 4:-4, 4:-4] - neighbours(padded)

def closure(w_first, w_second, w_third, inputs):
    linear_first = jnp.dot(w_first, inputs, preferred_element_type=jnp.float32)
    hidden_first = jax.nn.silu(linear_first).astype(jnp.bfloat16)
    linear_second = jnp.dot(w_second, hidden_first, preferred_element_type=jnp.float32)
    hidden_second = jax.nn.silu(linear_second).astype(jnp.bfloat16)
    predicted = jnp.dot(w_third, hidden_second, preferred_element_type=jnp.float32)
    return (linear_first, hidden_first, linear_second, hidden_second, predicted)

def slope(linear):
    sigmoid = jax.nn.sigmoid(linear)
    return sigmoid * (1.0 + linear * (1.0 - sigmoid))

def gradients(w_first, w_second, w_third, inputs, targets):
    linear_first, hidden_first, linear_second, hidden_second, predicted = closure(w_first, w_second, w_third, inputs)
    error = (predicted - targets.astype(jnp.float32)).astype(jnp.bfloat16)
    contract = (((1,), (1,)), ((), ()))
    leading = (((0,), (0,)), ((), ()))
    grad_third = lax.dot_general(error, hidden_second, contract, preferred_element_type=jnp.float32)
    back_second = lax.dot_general(w_third, error, leading, preferred_element_type=jnp.float32)
    delta_second = (back_second * slope(linear_second)).astype(jnp.bfloat16)
    grad_second = lax.dot_general(delta_second, hidden_first, contract, preferred_element_type=jnp.float32)
    back_first = lax.dot_general(w_second, delta_second, leading, preferred_element_type=jnp.float32)
    delta_first = (back_first * slope(linear_first)).astype(jnp.bfloat16)
    grad_first = lax.dot_general(delta_first, inputs, contract, preferred_element_type=jnp.float32)
    return (grad_first, grad_second, grad_third)

def normalize(gradient):
    return gradient * lax.rsqrt(jnp.mean(gradient * gradient) + epsilon)

def reference(right_side, diagonal, element_features, sample_bank, target_bank, patch_index, w_first, w_second, w_third):
    predicted = closure(w_first, w_second, w_third, element_features)[4]
    trace = (predicted[0] + predicted[1] + predicted[2]) / 3.0
    elems_x = CX // EL
    elems_y = CY // EL
    elems_z = CZ // EL
    blocks = trace.reshape(N_GX, N_GZ, N_GA, elems_x, elems_y, elems_z)
    blocks = blocks.transpose(0, 3, 2, 4, 1, 5).reshape(N_GX * elems_x, N_GA * elems_y, N_GZ * elems_z)
    forcing = jnp.repeat(jnp.repeat(jnp.repeat(blocks, EL, 0), EL, 1), EL, 2)
    source = right_side + forcing
    precond = diagonal + center
    pressure = jnp.zeros_like(source)
    residual = source
    scaled = residual / precond
    direction = scaled
    product_now = jnp.sum(residual * scaled)
    for iteration in range(ITERS):
        image_dir = operate(jnp.pad(direction, 4), precond)
        step_len = product_now / jnp.sum(direction * image_dir)
        pressure = pressure + step_len * direction
        residual = residual - step_len * image_dir
        scaled = residual / precond
        product_next = jnp.sum(residual * scaled)
        direction = scaled + product_next / product_now * direction
        product_now = product_next

    def accumulate(device, running):
        sample_start = (device * SAMPLES_DEV).astype(jnp.int32)
        bank_start = (device * BANK_DEV).astype(jnp.int32)
        columns = lax.dynamic_slice_in_dim(patch_index, sample_start, SAMPLES_DEV)
        bank_shard = lax.dynamic_slice_in_dim(sample_bank, bank_start, BANK_DEV, 1)
        goal_shard = lax.dynamic_slice_in_dim(target_bank, bank_start, BANK_DEV, 1)
        inputs = jnp.take(bank_shard, columns, axis=1)
        targets = jnp.take(goal_shard, columns, axis=1)
        partial_value = gradients(w_first, w_second, w_third, inputs, targets)
        return tuple((before + after for before, after in zip(running, partial_value)))
    initial = (jnp.zeros((CH, CH), jnp.float32), jnp.zeros((CH, CH), jnp.float32), jnp.zeros((STRESS, CH), jnp.float32))
    grad_first, grad_second, grad_third = lax.fori_loop(0, N_GX * N_GZ * N_GA, accumulate, initial)
    return (pressure, residual, normalize(grad_first), normalize(grad_second), normalize(grad_third))
```

```python
import functools

import jax
import jax.numpy as jnp
from jax import lax
from jax.experimental import pallas as pl
from jax.experimental.pallas import tpu as pltpu
from jax.sharding import Mesh
from jax.sharding import PartitionSpec as P

EL = 8
BLOCKS = (4, 4, 4)
GX = ("gx_0", "gx_1", "gx_2")
GX_GZ_GA = ("gx_0", "gx_1", "gx_2", "gz", "ga")

taps = (1.6, -0.2, 8.0 / 315.0, -1.0 / 560.0)
center = 3.0 * 205.0 / 72.0
epsilon = 1e-06
MIDDLE = 1.075
HALF = 0.925
THIRD_AT = 64
EXACT = lax.Precision.HIGHEST
F32 = jnp.float32
VMEM = pl.BlockSpec(memory_space=pltpu.VMEM)


def call(kernel, out_shapes, scratch, *args):
    return pl.pallas_call(
        kernel,
        out_shape=[jax.ShapeDtypeStruct(s, F32) for s in out_shapes],
        in_specs=[VMEM] * len(args),
        out_specs=[VMEM] * len(out_shapes),
        scratch_shapes=[pltpu.VMEM(s, F32) for s in scratch],
        compiler_params=pltpu.CompilerParams(vmem_limit_bytes=48 * 1024 * 1024),
    )(*args)


def pairs(count, odd):
    found = []
    for a in range(odd, count, 2):
        b = (a + 1) % count
        found += [(a, b), (b, a)]
    return found


def exchange(faces):
    xa, xb, ya, yb, za, zb = faces
    nx, ny, nz = lax.axis_size(GX), lax.axis_size("ga"), lax.axis_size("gz")
    return (
        lax.ppermute(xa, GX, pairs(nx, 0)),
        lax.ppermute(xb, GX, pairs(nx, 1)),
        lax.ppermute(ya, "ga", pairs(ny, 0)),
        lax.ppermute(yb, "ga", pairs(ny, 1)),
        lax.ppermute(za, "gz", pairs(nz, 0)),
        lax.ppermute(zb, "gz", pairs(nz, 1)),
    )


def tap_of(distance):
    distance = jnp.abs(distance)
    value = jnp.zeros(distance.shape, F32)
    for offset in range(1, 5):
        value = jnp.where(distance == offset, F32(taps[offset - 1]), value)
    return value


FLAGS, SELECT, SPREAD, BAND = 0, 8, 24, 40


def tables():
    rows = []
    even = {}
    inner = {}
    for name, axis in (("x", GX), ("y", "ga"), ("z", "gz")):
        index, count = lax.axis_index(axis), lax.axis_size(axis)
        even[name] = index % 2 == 0
        inner[name] = (index != 0) & (index != count - 1)
        rows += [even[name], inner[name]]
    rows += [even["x"], even["x"]]
    flags = jnp.broadcast_to(jnp.stack(rows).astype(F32)[:, None], (8, 128))
    row = lax.broadcasted_iota(jnp.int32, (16, 128), 0)
    lane = lax.broadcasted_iota(jnp.int32, (16, 128), 1)
    inside = row % 8
    upper = (row < 8) == even["z"]
    used = inside < 4
    select = jnp.where(used & (lane == inside + jnp.where(upper, 124, 0)), 1.0, 0.0)
    place = inside + jnp.where(upper, 128, -4)
    allowed = used & ((row < 8) | inner["z"])
    spread = jnp.where(allowed, tap_of(lane - place), 0.0)
    out = lax.broadcasted_iota(jnp.int32, (128, 128), 0)
    within = lax.broadcasted_iota(jnp.int32, (128, 128), 1)
    return jnp.concatenate([flags, select, spread, tap_of(out - within)], axis=0)


FACES = ((4, 32, 128), (4, 32, 128), (16, 4, 128), (16, 4, 128), (8, 512), (8, 512))
GRID = (16, 32, 128)


def write_faces(table, field, faces):
    xa, xb, ya, yb, za, zb = faces
    even_x = table[0:1, :] > 0.5
    even_y = table[2:3, :] > 0.5
    xa[...] = jnp.where(even_x, field[12:16], field[0:4])
    xb[...] = jnp.where(even_x, field[0:4], field[12:16])
    ya[...] = jnp.where(even_y, field[:, 28:32, :], field[:, 0:4, :])
    yb[...] = jnp.where(even_y, field[:, 0:4, :], field[:, 28:32, :])
    flat = field[...].reshape(512, 128)
    both = lax.dot_general(
        table[SELECT : SELECT + 16, :], flat, (((1,), (1,)), ((), ())),
        precision=EXACT, preferred_element_type=F32,
    )
    za[...] = both[0:8]
    zb[...] = both[8:16]


def image_planes(table, field, halo, xs, ys, zs, use):
    xa, xb, ya, yb, za, zb = halo
    even_x = table[0:1, :] > 0.5
    keep_x = table[1:2, :] > 0.5
    even_y = table[2:3, :] > 0.5
    keep_y = table[3:4, :] > 0.5
    outer = jnp.where(keep_x, xb[...], 0.0)
    xs[0:4] = jnp.where(even_x, outer, xa[...])
    xs[4:8] = jnp.where(even_x, xa[...], outer)
    outer = jnp.where(keep_y, yb[...], 0.0)
    ys[:, 4:8, :] = jnp.where(even_y, outer, ya[...])
    ys[:, 40:44, :] = jnp.where(even_y, ya[...], outer)
    ys[:, 8:40, :] = field[...]
    flat = field[...].reshape(512, 128)
    arrived = jnp.concatenate([za[...], zb[...]], axis=0)
    zs[...] = jnp.dot(
        flat, table[BAND : BAND + 128, :], precision=EXACT, preferred_element_type=F32
    ) + lax.dot_general(
        arrived, table[SPREAD : SPREAD + 16, :], (((0,), (0,)), ((), ())),
        precision=EXACT, preferred_element_type=F32,
    )

    def plane(i):
        if i < 0:
            return xs[i + 4]
        if i >= 16:
            return xs[i - 12]
        return field[i]

    for i in range(16):
        total = zs[32 * i : 32 * i + 32, :]
        for k in range(1, 5):
            along = (plane(i + k) + plane(i - k)) + (
                ys[i, 8 + k : 40 + k, :] + ys[i, 8 - k : 40 - k, :]
            )
            total = total + taps[k - 1] * along
        use(i, total)


HALO_SCRATCH = ((8, 32, 128), (16, 48, 128), (512, 128))


def start_kernel(table, right, diag, feats, w1, w2, w3, *rest):
    source, precond, inverse, basis = rest[:4]
    faces = rest[4:10]
    hidden = jnp.dot(w1[...], feats[...], preferred_element_type=F32)
    hidden = jax.nn.silu(hidden).astype(jnp.bfloat16)
    hidden = jnp.dot(w2[...], hidden, preferred_element_type=F32)
    hidden = jax.nn.silu(hidden).astype(jnp.bfloat16)
    stress = jnp.dot(w3[...], hidden, preferred_element_type=F32)
    trace = (stress[0:1] + stress[1:2] + stress[2:3]) / 3.0
    row = lax.broadcasted_iota(jnp.int32, (8, 128), 0)
    lane = lax.broadcasted_iota(jnp.int32, (8, 128), 1)
    apart = jnp.where(lane // 16 == row, trace, 0.0)
    element = lax.broadcasted_iota(jnp.int32, (128, 128), 0)
    node = lax.broadcasted_iota(jnp.int32, (128, 128), 1)
    widen = jnp.where(element % 16 == node // EL, 1.0, 0.0)
    wide = jnp.dot(apart, widen, precision=EXACT, preferred_element_type=F32)
    for i in range(16):
        for j in range(4):
            at = (i // EL) * 4 + j
            rows = slice(EL * j, EL * j + EL)
            value = right[i, rows, :] + wide[at : at + 1, :]
            weight = diag[i, rows, :] + center
            source[i, rows, :] = value
            precond[i, rows, :] = weight
            inverted = 1.0 / weight
            inverse[i, rows, :] = inverted
            basis[i, rows, :] = value * inverted
    write_faces(table, basis, faces)


def step_kernel(first, table, field, before, precond, inverse, *rest):
    halo, rest = rest[:6], rest[6:]
    image, after = rest[:2]
    faces, scratch = rest[2:8], rest[8:]

    def use(i, total):
        value = field[i]
        image[i] = precond[i] * value - total
        if first:
            after[i] = ((1.0 - MIDDLE) * value - total * inverse[i]) * (1.0 / HALF)
        else:
            after[i] = ((1.0 - MIDDLE) * value - total * inverse[i]) * (2.0 / HALF) - before[i]

    image_planes(table, field, halo, *scratch, use)
    write_faces(table, after, faces)


def products(size, old):
    wanted = [(("t", i), ("q", j)) for i in range(size) for j in range(i, size)]
    wanted += [(("t", i), ("r", 0)) for i in range(size)]
    groups = [wanted]
    if old:
        for i0 in range(0, old, 4):
            groups.append([(("p", i), ("q", j)) for i in range(i0, min(old, i0 + 4)) for j in range(size)])
    return groups


def last_kernel(size, old, table, precond, residual, *rest):
    halo, rest = rest[:6], rest[6:]
    basis, rest = rest[:size], rest[size:]
    images, rest = rest[: size - 1], rest[size - 1 :]
    olds, rest = rest[:old], rest[old:]
    image, row = rest[:2]
    scratch, sums = rest[2:5], rest[5]
    field = basis[-1]

    def use(i, total):
        image[i] = precond[i] * field[i] - total

    image_planes(table, field, halo, *scratch, use)
    refs = {("r", 0): residual}
    for j in range(size):
        refs["t", j] = basis[j]
        refs["q", j] = images[j] if j < size - 1 else image
    for j in range(old):
        refs["p", j] = olds[j]
    sums[...] = jnp.zeros(sums.shape, F32)
    at = 0
    for group in products(size, old):
        names = sorted({name for pair in group for name in pair})

        def add(i, totals, names=names, group=group):
            for part in range(4):
                value = {n: refs[n][i, 8 * part : 8 * part + 8, :] for n in names}
                totals = tuple(
                    total + value[a] * value[b] for total, (a, b) in zip(totals, group)
                )
            return totals

        totals = lax.fori_loop(0, 16, add, (jnp.zeros((8, 128), F32),) * len(group))
        for total in totals:
            sums[at : at + 1, :] = jnp.sum(total, axis=0, keepdims=True)
            at += 1
    packed = lax.dot_general(
        jnp.ones((8, 128), F32), sums[...], (((1,), (1,)), ((), ())),
        precision=EXACT, preferred_element_type=F32,
    )
    for i in range(row.shape[0] // 8):
        row[8 * i : 8 * i + 8, :] = packed


def factor(matrix, size):
    low, scaled, inverse = {}, {}, []
    for j in range(size):
        pivot = matrix[j][j]
        for k in range(j):
            pivot = pivot - low[j, k] * scaled[j, k]
        inverse.append(1.0 / pivot)
        for i in range(j + 1, size):
            value = matrix[i][j]
            for k in range(j):
                value = value - scaled[i, k] * low[j, k]
            scaled[i, j] = value
            low[i, j] = value * inverse[j]
    return low, inverse


def solve(factors, size, right):
    low, inverse = factors
    found = []
    for i in range(size):
        value = right[i]
        for k in range(i):
            value = value - low[i, k] * found[k]
        found.append(value)
    found = [a * b for a, b in zip(found, inverse)]
    for i in reversed(range(size)):
        for k in range(i + 1, size):
            found[i] = found[i] - low[k, i] * found[k]
    return found


def update_kernel(size, old, final, *rest):
    gathered, table, residual, rest = rest[0], rest[1], rest[2], rest[3:]
    basis, rest = rest[:size], rest[size:]
    images, rest = rest[:size], rest[size:]
    if old:
        pressure, weights, rest = rest[0], rest[1], rest[2:]
        old_basis, rest = rest[:old], rest[old:]
        old_images, rest = rest[:old], rest[old:]
    if not final:
        inverse, rest = rest[0], rest[1:]
    new_pressure, new_residual = rest[:2]
    rest = rest[2:]
    if not final:
        after, faces, new_weights, rest = rest[0], rest[1:7], rest[7], rest[8:]
        if old:
            new_basis, rest = rest[:size], rest[size:]
            new_images, rest = rest[:size], rest[size:]
    splats = rest[0]
    totals = jnp.sum(gathered[...], axis=0, keepdims=True)
    row = lax.broadcasted_iota(jnp.int32, (128, 128), 0)
    lane = lax.broadcasted_iota(jnp.int32, (128, 128), 1)
    splats[...] = jnp.dot(
        jnp.where((row == lane) & (lane < THIRD_AT), totals, 0.0), jnp.ones((128, 128), F32),
        precision=EXACT, preferred_element_type=F32,
    )
    value = {}
    at = 0
    for group in products(size, old):
        for a, b in group:
            value[a, b] = splats[at : at + 1, :]
            at += 1
    gram = [[value[("t", min(i, j)), ("q", max(i, j))] for j in range(size)] for i in range(size)]
    right = [value[("t", i), ("r", 0)] for i in range(size)]
    mix = None
    if old:
        cross = [[value[("p", i), ("q", j)] for j in range(size)] for i in range(old)]
        held = [[weights[i * old + j : i * old + j + 1, :] for j in range(old)] for i in range(old)]
        factors = factor(held, old)
        columns = [solve(factors, old, [-cross[i][j] for i in range(old)]) for j in range(size)]
        for i in range(size):
            for j in range(i, size):
                for k in range(old):
                    gram[i][j] = gram[i][j] + cross[k][i] * columns[j][k]
                gram[j][i] = gram[i][j]
        mix = [[jnp.broadcast_to(v, (8, 128)) for v in column] for column in columns]
    step = solve(factor(gram, size), size, right)
    if not final:
        new_weights[...] = jnp.zeros(new_weights.shape, F32)
        for i in range(size):
            for j in range(size):
                new_weights[i * size + j : i * size + j + 1, :] = gram[i][j]
    if old and final:
        carried = []
        for i in range(old):
            total = step[0] * columns[0][i]
            for j in range(1, size):
                total = total + step[j] * columns[j][i]
            carried.append(jnp.broadcast_to(total, (8, 128)))
    step = [jnp.broadcast_to(v, (8, 128)) for v in step]

    def tile(i, part):
        rows = slice(8 * part, 8 * part + 8)
        vectors = [ref[i, rows, :] for ref in basis]
        duals = [ref[i, rows, :] for ref in images]
        if old and not final:
            held_v = [ref[i, rows, :] for ref in old_basis]
            held_d = [ref[i, rows, :] for ref in old_images]
            for j in range(size):
                for k in range(old):
                    vectors[j] = vectors[j] + mix[j][k] * held_v[k]
                    duals[j] = duals[j] + mix[j][k] * held_d[k]
                new_basis[j][i, rows, :] = vectors[j]
                new_images[j][i, rows, :] = duals[j]
        gain = step[0] * vectors[0]
        loss = step[0] * duals[0]
        for j in range(1, size):
            gain = gain + step[j] * vectors[j]
            loss = loss + step[j] * duals[j]
        if old and final:
            for k in range(old):
                gain = gain + carried[k] * old_basis[k][i, rows, :]
                loss = loss + carried[k] * old_images[k][i, rows, :]
        if old:
            gain = pressure[i, rows, :] + gain
        left = residual[i, rows, :] - loss
        new_pressure[i, rows, :] = gain
        new_residual[i, rows, :] = left
        if not final:
            after[i, rows, :] = left * inverse[i, rows, :]

    def planes(i, nothing):
        for part in range(4):
            tile(i, part)
        return nothing

    lax.fori_loop(0, 16, planes, 0)
    if not final:
        write_faces(table, after, faces)


def all_rows(rows):
    return lax.all_to_all(rows, GX_GZ_GA, split_axis=0, concat_axis=0, tiled=True)


def closure(w_first, w_second, w_third, inputs):
    linear_first = jnp.dot(w_first, inputs, preferred_element_type=F32)
    hidden_first = jax.nn.silu(linear_first).astype(jnp.bfloat16)
    linear_second = jnp.dot(w_second, hidden_first, preferred_element_type=F32)
    hidden_second = jax.nn.silu(linear_second).astype(jnp.bfloat16)
    predicted = jnp.dot(w_third, hidden_second, preferred_element_type=F32)
    return (linear_first, hidden_first, linear_second, hidden_second, predicted)


def slope(linear):
    sigmoid = jax.nn.sigmoid(linear)
    return sigmoid * (1.0 + linear * (1.0 - sigmoid))


def gradients(w_first, w_second, w_third, inputs, targets):
    linear_first, hidden_first, linear_second, hidden_second, predicted = closure(
        w_first, w_second, w_third, inputs
    )
    error = (predicted - targets.astype(F32)).astype(jnp.bfloat16)
    contract = (((1,), (1,)), ((), ()))
    leading = (((0,), (0,)), ((), ()))
    grad_third = lax.dot_general(error, hidden_second, contract, preferred_element_type=F32)
    back_second = lax.dot_general(w_third, error, leading, preferred_element_type=F32)
    delta_second = (back_second * slope(linear_second)).astype(jnp.bfloat16)
    grad_second = lax.dot_general(delta_second, hidden_first, contract, preferred_element_type=F32)
    back_first = lax.dot_general(w_second, delta_second, leading, preferred_element_type=F32)
    delta_first = (back_first * slope(linear_first)).astype(jnp.bfloat16)
    grad_first = lax.dot_general(delta_first, inputs, contract, preferred_element_type=F32)
    return (grad_first, grad_second, grad_third)


def normalize(gradient):
    return gradient * lax.rsqrt(jnp.mean(gradient * gradient) + epsilon)


def body(
    right_side,
    diagonal,
    element_features,
    sample_bank,
    target_bank,
    patch_index,
    w_first,
    w_second,
    w_third,
):
    devices = lax.axis_size(GX_GZ_GA)
    table = tables()
    inputs = jnp.take(sample_bank, patch_index, axis=1)
    targets = jnp.take(target_bank, patch_index, axis=1)
    grad_first, grad_second, grad_third = gradients(w_first, w_second, w_third, inputs, targets)
    half = 128
    stacked = jnp.concatenate(
        (grad_first[:, :half], grad_first[:, half:], grad_second[:, :half], grad_second[:, half:]), axis=0
    ).reshape(devices, -1, half)
    third_size = grad_third.size // devices
    third_rows = jnp.pad(
        grad_third.reshape(devices, third_size), ((0, 0), (THIRD_AT, half - THIRD_AT - third_size))
    )

    residual, precond, inverse, vector, *faces = call(
        start_kernel, (GRID,) * 4 + FACES, (), table, right_side, diagonal, element_features,
        w_first, w_second, w_third,
    )
    pressure = None
    weights, old_basis, old_images = None, [], []
    for number, size in enumerate(BLOCKS):
        final = number + 1 == len(BLOCKS)
        old = len(old_basis)
        basis, images = [vector], []
        for j in range(size - 1):
            halo = exchange(faces)
            image, vector, *faces = call(
                functools.partial(step_kernel, j == 0), (GRID, GRID) + FACES, HALO_SCRATCH,
                table, basis[-1], basis[max(j - 1, 0)], precond, inverse, *halo,
            )
            basis.append(vector)
            images.append(image)
        halo = exchange(faces)
        image, rows = call(
            functools.partial(last_kernel, size, old), (GRID, (devices, 128)), HALO_SCRATCH + ((128, 128),),
            table, precond, residual, *halo, *basis, *images, *old_basis,
        )
        images.append(image)
        if number == len(BLOCKS) - 2:
            rows = rows + third_rows
        if final:
            rows = rows + third_share
        rows = all_rows(rows)
        if number == len(BLOCKS) - 2:
            lane = lax.broadcasted_iota(jnp.int32, (1, 128), 1)
            third_share = jnp.where(lane < THIRD_AT, 0.0, jnp.sum(rows, axis=0, keepdims=True))
        given = [rows, table, residual, *basis, *images]
        shapes = [GRID, GRID]
        if old:
            given += [pressure, weights, *old_basis, *old_images]
        if not final:
            given += [inverse]
            shapes += [GRID, *FACES, (64, 128)]
            if old:
                shapes += [GRID] * (2 * size)
        pressure, residual, *more = call(
            functools.partial(update_kernel, size, old, final), shapes, ((128, 128),), *given
        )
        if not final:
            vector, faces, weights = more[0], more[1:7], more[7]
            old_basis, old_images = basis, images
            if old:
                old_basis, old_images = more[8 : 8 + size], more[8 + size :]
    third = rows[:, THIRD_AT : THIRD_AT + third_size].reshape(grad_third.shape)

    share = jnp.sum(all_rows(stacked), axis=0, keepdims=True)
    whole = all_rows(jnp.broadcast_to(share, (devices, *share.shape[1:]))).reshape(-1, half)
    channels = w_first.shape[0]
    whole = [whole[channels * i : channels * i + channels] for i in range(4)]
    first = jnp.concatenate(whole[:2], axis=1)
    second = jnp.concatenate(whole[2:], axis=1)
    return (pressure, residual, normalize(first), normalize(second), normalize(third))


def solution(mesh):
    finer = Mesh(
        mesh.devices.reshape(4, 2, 2, mesh.shape["gz"], mesh.shape["ga"]),
        GX_GZ_GA,
    )
    return jax.shard_map(
        body,
        mesh=finer,
        in_specs=(
            P(GX, "ga", "gz"),
            P(GX, "ga", "gz"),
            P(None, GX_GZ_GA),
            P(None, GX_GZ_GA),
            P(None, GX_GZ_GA),
            P(GX_GZ_GA),
            P(),
            P(),
            P(),
        ),
        out_specs=(P(GX, "ga", "gz"), P(GX, "ga", "gz"), P(), P(), P()),
        check_vma=False,
    )
```

```python
import functools

import jax
import jax.numpy as jnp
from jax import lax
from jax.experimental import pallas as pl
from jax.experimental.pallas import tpu as pltpu
from jax.sharding import Mesh
from jax.sharding import PartitionSpec as P

EL = 8
BLOCKS = (6, 6)
GROUPS = 4
GX = ("gx_0", "gx_1", "gx_2")
GX_GZ_GA = ("gx_0", "gx_1", "gx_2", "gz", "ga")

taps = (1.6, -0.2, 8.0 / 315.0, -1.0 / 560.0)
center = 3.0 * 205.0 / 72.0
epsilon = 1e-06
MIDDLE = 1.075
HALF = 0.925
THIRD_AT = 112
EXACT = lax.Precision.HIGHEST
F32 = jnp.float32
VMEM = pl.BlockSpec(memory_space=pltpu.VMEM)


def call(kernel, out_shapes, scratch, *args, room=14, aliases={}):
    return pl.pallas_call(
        kernel,
        out_shape=[jax.ShapeDtypeStruct(s, F32) for s in out_shapes],
        in_specs=[VMEM] * len(args),
        out_specs=[VMEM] * len(out_shapes),
        scratch_shapes=[pltpu.VMEM(s, F32) for s in scratch],
        input_output_aliases=aliases,
        compiler_params=pltpu.CompilerParams(vmem_limit_bytes=room * 1024 * 1024),
    )(*args)


def pairs(count, odd):
    found = []
    for a in range(odd, count, 2):
        b = (a + 1) % count
        found += [(a, b), (b, a)]
    return found


def exchange(faces):
    xa, xb, ya, yb, za, zb = faces
    nx, ny, nz = lax.axis_size(GX), lax.axis_size("ga"), lax.axis_size("gz")
    return (
        lax.ppermute(xa, GX, pairs(nx, 0)),
        lax.ppermute(xb, GX, pairs(nx, 1)),
        lax.ppermute(ya, "ga", pairs(ny, 0)),
        lax.ppermute(yb, "ga", pairs(ny, 1)),
        lax.ppermute(za, "gz", pairs(nz, 0)),
        lax.ppermute(zb, "gz", pairs(nz, 1)),
    )


def tap_of(distance):
    distance = jnp.abs(distance)
    value = jnp.zeros(distance.shape, F32)
    for offset in range(1, 5):
        value = jnp.where(distance == offset, F32(taps[offset - 1]), value)
    return value


FLAGS, SELECT, SPREAD, BAND = 0, 8, 24, 40


def tables():
    rows = []
    even = {}
    inner = {}
    for name, axis in (("x", GX), ("y", "ga"), ("z", "gz")):
        index, count = lax.axis_index(axis), lax.axis_size(axis)
        even[name] = index % 2 == 0
        inner[name] = (index != 0) & (index != count - 1)
        rows += [even[name], inner[name]]
    rows += [even["x"], even["x"]]
    flags = jnp.broadcast_to(jnp.stack(rows).astype(F32)[:, None], (8, 128))
    row = lax.broadcasted_iota(jnp.int32, (16, 128), 0)
    lane = lax.broadcasted_iota(jnp.int32, (16, 128), 1)
    inside = row % 8
    upper = (row < 8) == even["z"]
    used = inside < 4
    select = jnp.where(used & (lane == inside + jnp.where(upper, 124, 0)), 1.0, 0.0)
    place = inside + jnp.where(upper, 128, -4)
    allowed = used & ((row < 8) | inner["z"])
    spread = jnp.where(allowed, tap_of(lane - place), 0.0)
    out = lax.broadcasted_iota(jnp.int32, (128, 128), 0)
    within = lax.broadcasted_iota(jnp.int32, (128, 128), 1)
    return jnp.concatenate([flags, select, spread, tap_of(out - within)], axis=0)


FACES = ((4, 32, 128), (4, 32, 128), (16, 4, 128), (16, 4, 128), (8, 512), (8, 512))
GRID = (16, 32, 128)


def write_faces(table, field, faces):
    xa, xb, ya, yb, za, zb = faces
    even_x = table[0:1, :] > 0.5
    even_y = table[2:3, :] > 0.5
    xa[...] = jnp.where(even_x, field[12:16], field[0:4])
    xb[...] = jnp.where(even_x, field[0:4], field[12:16])
    ya[...] = jnp.where(even_y, field[:, 28:32, :], field[:, 0:4, :])
    yb[...] = jnp.where(even_y, field[:, 0:4, :], field[:, 28:32, :])
    flat = field[...].reshape(512, 128)
    both = lax.dot_general(
        table[SELECT : SELECT + 16, :], flat, (((1,), (1,)), ((), ())),
        precision=EXACT, preferred_element_type=F32,
    )
    za[...] = both[0:8]
    zb[...] = both[8:16]


def image_planes(table, field, halo, xs, ys, zs, use):
    xa, xb, ya, yb, za, zb = halo
    even_x = table[0:1, :] > 0.5
    keep_x = table[1:2, :] > 0.5
    even_y = table[2:3, :] > 0.5
    keep_y = table[3:4, :] > 0.5
    outer = jnp.where(keep_x, xb[...], 0.0)
    xs[0:4] = jnp.where(even_x, outer, xa[...])
    xs[4:8] = jnp.where(even_x, xa[...], outer)
    outer = jnp.where(keep_y, yb[...], 0.0)
    ys[:, 4:8, :] = jnp.where(even_y, outer, ya[...])
    ys[:, 40:44, :] = jnp.where(even_y, ya[...], outer)
    ys[:, 8:40, :] = field[...]
    flat = field[...].reshape(512, 128)
    arrived = jnp.concatenate([za[...], zb[...]], axis=0)
    zs[...] = jnp.dot(
        flat, table[BAND : BAND + 128, :], precision=EXACT, preferred_element_type=F32
    ) + lax.dot_general(
        arrived, table[SPREAD : SPREAD + 16, :], (((0,), (0,)), ((), ())),
        precision=EXACT, preferred_element_type=F32,
    )

    def plane(i):
        if i < 0:
            return xs[i + 4]
        if i >= 16:
            return xs[i - 12]
        return field[i]

    for i in range(16):
        total = zs[32 * i : 32 * i + 32, :]
        for k in range(1, 5):
            along = (plane(i + k) + plane(i - k)) + (
                ys[i, 8 + k : 40 + k, :] + ys[i, 8 - k : 40 - k, :]
            )
            total = total + taps[k - 1] * along
        use(i, total)


HALO_SCRATCH = ((8, 32, 128), (16, 48, 128), (512, 128))


def start_kernel(table, right, diag, feats, w1, w2, w3, *rest):
    source, precond, inverse, basis = rest[:4]
    faces = rest[4:10]
    hidden = jnp.dot(w1[...], feats[...], preferred_element_type=F32)
    hidden = jax.nn.silu(hidden).astype(jnp.bfloat16)
    hidden = jnp.dot(w2[...], hidden, preferred_element_type=F32)
    hidden = jax.nn.silu(hidden).astype(jnp.bfloat16)
    stress = jnp.dot(w3[...], hidden, preferred_element_type=F32)
    trace = (stress[0:1] + stress[1:2] + stress[2:3]) / 3.0
    row = lax.broadcasted_iota(jnp.int32, (8, 128), 0)
    lane = lax.broadcasted_iota(jnp.int32, (8, 128), 1)
    apart = jnp.where(lane // 16 == row, trace, 0.0)
    element = lax.broadcasted_iota(jnp.int32, (128, 128), 0)
    node = lax.broadcasted_iota(jnp.int32, (128, 128), 1)
    widen = jnp.where(element % 16 == node // EL, 1.0, 0.0)
    wide = jnp.dot(apart, widen, precision=EXACT, preferred_element_type=F32)
    for i in range(16):
        for j in range(4):
            at = (i // EL) * 4 + j
            rows = slice(EL * j, EL * j + EL)
            value = right[i, rows, :] + wide[at : at + 1, :]
            weight = diag[i, rows, :] + center
            source[i, rows, :] = value
            precond[i, rows, :] = weight
            inverted = 1.0 / weight
            inverse[i, rows, :] = inverted
            basis[i, rows, :] = value * inverted
    write_faces(table, basis, faces)


def step_kernel(first, table, field, before, precond, inverse, *rest):
    halo, rest = rest[:6], rest[6:]
    image, after = rest[:2]
    faces, scratch = rest[2:8], rest[8:]

    def use(i, total):
        value = field[i]
        image[i] = precond[i] * value - total
        if first:
            after[i] = ((1.0 - MIDDLE) * value - total * inverse[i]) * (1.0 / HALF)
        else:
            after[i] = ((1.0 - MIDDLE) * value - total * inverse[i]) * (2.0 / HALF) - before[i]

    image_planes(table, field, halo, *scratch, use)
    write_faces(table, after, faces)


def products(size, old):
    wanted = [(("t", i), ("q", j)) for i in range(size) for j in range(i, size)]
    wanted += [(("t", i), ("r", 0)) for i in range(size)]
    groups = [wanted]
    if old:
        for i0 in range(0, old, 4):
            some = range(i0, min(old, i0 + 4))
            groups.append([(("p", i), ("q", j)) for i in some for j in range(size)] + [(("p", i), ("r", 0)) for i in some])
    return groups


def last_kernel(size, old, table, precond, residual, extra, *rest):
    halo, rest = rest[:6], rest[6:]
    basis, rest = rest[:size], rest[size:]
    images, rest = rest[: size - 1], rest[size - 1 :]
    olds, rest = rest[:old], rest[old:]
    image, row = rest[:2]
    scratch, sums = rest[2:5], rest[5]
    field = basis[-1]

    def use(i, total):
        image[i] = precond[i] * field[i] - total

    image_planes(table, field, halo, *scratch, use)
    refs = {("r", 0): residual}
    for j in range(size):
        refs["t", j] = basis[j]
        refs["q", j] = images[j] if j < size - 1 else image
    for j in range(old):
        refs["p", j] = olds[j]
    sums[...] = jnp.zeros(sums.shape, F32)
    at = 0
    for group in products(size, old):
        names = sorted({name for pair in group for name in pair})

        def add(i, totals, names=names, group=group):
            for part in range(4):
                value = {n: refs[n][i, 8 * part : 8 * part + 8, :] for n in names}
                totals = tuple(
                    total + value[a] * value[b] for total, (a, b) in zip(totals, group)
                )
            return totals

        totals = lax.fori_loop(0, 16, add, (jnp.zeros((8, 128), F32),) * len(group))
        for total in totals:
            sums[at : at + 1, :] = jnp.sum(total, axis=0, keepdims=True)
            at += 1
    packed = lax.dot_general(
        jnp.ones((8, 128), F32), sums[...], (((1,), (1,)), ((), ())),
        precision=EXACT, preferred_element_type=F32,
    )
    shared = extra.shape[0] == 8
    for i in range(row.shape[0] // 8):
        rows = slice(8 * i, 8 * i + 8)
        row[rows, :] = packed + (extra[...] if shared else extra[rows, :])


def factor(matrix, size):
    low, scaled, inverse = {}, {}, []
    for j in range(size):
        pivot = matrix[j][j]
        for k in range(j):
            pivot = pivot - low[j, k] * scaled[j, k]
        inverse.append(1.0 / pivot)
        for i in range(j + 1, size):
            value = matrix[i][j]
            for k in range(j):
                value = value - scaled[i, k] * low[j, k]
            scaled[i, j] = value
            low[i, j] = value * inverse[j]
    return low, inverse


def solve(factors, size, right):
    low, inverse = factors
    found = []
    for i in range(size):
        value = right[i]
        for k in range(i):
            value = value - low[i, k] * found[k]
        found.append(value)
    found = [a * b for a, b in zip(found, inverse)]
    for i in reversed(range(size)):
        for k in range(i + 1, size):
            found[i] = found[i] - low[k, i] * found[k]
    return found


def update_kernel(size, old, final, *rest):
    gathered, table, residual, rest = rest[0], rest[1], rest[2], rest[3:]
    basis, rest = rest[:size], rest[size:]
    images, rest = rest[:size], rest[size:]
    if old:
        pressure, weights, rest = rest[0], rest[1], rest[2:]
        old_basis, rest = rest[:old], rest[old:]
        old_images, rest = rest[:old], rest[old:]
    if not final:
        inverse, rest = rest[0], rest[1:]
    new_pressure, new_residual = rest[:2]
    rest = rest[2:]
    if final:
        third, rest = rest[0], rest[1:]
    else:
        after, faces, new_weights, share, rest = rest[0], rest[1:7], rest[7], rest[8], rest[9:]
        if old:
            new_basis, rest = rest[:size], rest[size:]
            new_images, rest = rest[:size], rest[size:]
    splats = rest[0]
    totals = jnp.sum(gathered[...], axis=0, keepdims=True)
    row = lax.broadcasted_iota(jnp.int32, (128, 128), 0)
    lane = lax.broadcasted_iota(jnp.int32, (128, 128), 1)
    splats[...] = jnp.dot(
        jnp.where((row == lane) & (lane < THIRD_AT), totals, 0.0), jnp.ones((128, 128), F32),
        precision=EXACT, preferred_element_type=F32,
    )
    if final:
        at_row = lax.broadcasted_iota(jnp.int32, (8, 128), 0)
        at_lane = lax.broadcasted_iota(jnp.int32, (8, 128), 1)
        taken = lax.dot_general(
            jnp.where((at_lane == at_row + THIRD_AT) & (at_row < third.shape[0]), 1.0, 0.0), gathered[...],
            (((1,), (1,)), ((), ())), precision=EXACT, preferred_element_type=F32,
        )
        square = jnp.sum(jnp.sum(taken * taken, axis=0, keepdims=True), axis=1, keepdims=True)
        taken = taken * lax.rsqrt(square / (third.shape[0] * third.shape[1]) + epsilon)
        third[...] = taken[: third.shape[0]]
    else:
        kept = jnp.where(lane[0:8] < THIRD_AT, 0.0, totals)
        share[...] = kept
    value = {}
    at = 0
    for group in products(size, old):
        for a, b in group:
            value[a, b] = splats[at : at + 1, :]
            at += 1
    gram = [[value[("t", min(i, j)), ("q", max(i, j))] for j in range(size)] for i in range(size)]
    right = [value[("t", i), ("r", 0)] for i in range(size)]
    mix = None
    if old:
        cross = [[value[("p", i), ("q", j)] for j in range(size)] for i in range(old)]
        held = [[weights[i * old + j : i * old + j + 1, :] for j in range(old)] for i in range(old)]
        factors = factor(held, old)
        columns = [solve(factors, old, [-cross[i][j] for i in range(old)]) for j in range(size)]
        behind = [value[("p", i), ("r", 0)] for i in range(old)]
        for j in range(size):
            for k in range(old):
                right[j] = right[j] + columns[j][k] * behind[k]
        behind = solve(factors, old, behind)
        for i in range(size):
            for j in range(i, size):
                for k in range(old):
                    gram[i][j] = gram[i][j] + cross[k][i] * columns[j][k]
                gram[j][i] = gram[i][j]
        mix = [[jnp.broadcast_to(v, (8, 128)) for v in column] for column in columns]
    step = solve(factor(gram, size), size, right)
    if not final:
        new_weights[...] = jnp.zeros(new_weights.shape, F32)
        for i in range(size):
            for j in range(size):
                new_weights[i * size + j : i * size + j + 1, :] = gram[i][j]
    if old:
        carried = []
        for i in range(old):
            total = behind[i]
            if final:
                for j in range(size):
                    total = total + step[j] * columns[j][i]
            carried.append(jnp.broadcast_to(total, (8, 128)))
    step = [jnp.broadcast_to(v, (8, 128)) for v in step]

    def tile(i, part):
        rows = slice(8 * part, 8 * part + 8)
        vectors = [ref[i, rows, :] for ref in basis]
        duals = [ref[i, rows, :] for ref in images]
        if old and not final:
            held_v = [ref[i, rows, :] for ref in old_basis]
            held_d = [ref[i, rows, :] for ref in old_images]
            for j in range(size):
                for k in range(old):
                    vectors[j] = vectors[j] + mix[j][k] * held_v[k]
                    duals[j] = duals[j] + mix[j][k] * held_d[k]
                new_basis[j][i, rows, :] = vectors[j]
                new_images[j][i, rows, :] = duals[j]
        gain = step[0] * vectors[0]
        loss = step[0] * duals[0]
        for j in range(1, size):
            gain = gain + step[j] * vectors[j]
            loss = loss + step[j] * duals[j]
        if old:
            for k in range(old):
                gain = gain + carried[k] * old_basis[k][i, rows, :]
                loss = loss + carried[k] * old_images[k][i, rows, :]
        if old:
            gain = pressure[i, rows, :] + gain
        left = residual[i, rows, :] - loss
        new_pressure[i, rows, :] = gain
        new_residual[i, rows, :] = left
        if not final:
            after[i, rows, :] = left * inverse[i, rows, :]

    def planes(i, nothing):
        for part in range(4):
            tile(i, part)
        return nothing

    lax.fori_loop(0, 16, planes, 0)
    if not final:
        write_faces(table, after, faces)


def all_rows(rows):
    return lax.all_to_all(rows, GX_GZ_GA, split_axis=0, concat_axis=0, tiled=True)


def slope_of(linear, sigmoid):
    return sigmoid * (1.0 + linear * (1.0 - sigmoid))


def learn_kernel(first, index, bank, target, w1, w2, w3, *rest):
    if not first:
        layers_in, third_in, rest = rest[0], rest[1], rest[2:]
    layers, third = rest
    group = index.shape[1]
    column = lax.broadcasted_iota(jnp.int32, (bank.shape[1], group), 0)
    chosen = jnp.where(column == index[...], 1.0, 0.0).astype(jnp.bfloat16)
    inputs = jnp.dot(bank[...], chosen, preferred_element_type=F32).astype(jnp.bfloat16)
    wanted = jnp.dot(target[...], chosen, preferred_element_type=F32)
    linear_1 = jnp.dot(w1[...], inputs, preferred_element_type=F32)
    sigmoid_1 = 1.0 / (1.0 + jnp.exp(-linear_1))
    hidden_1 = (linear_1 * sigmoid_1).astype(jnp.bfloat16)
    linear_2 = jnp.dot(w2[...], hidden_1, preferred_element_type=F32)
    sigmoid_2 = 1.0 / (1.0 + jnp.exp(-linear_2))
    hidden_2 = (linear_2 * sigmoid_2).astype(jnp.bfloat16)
    stress = jnp.dot(w3[...], hidden_2, preferred_element_type=F32)
    error = (stress - wanted).astype(jnp.bfloat16)
    contract = (((1,), (1,)), ((), ()))
    leading = (((0,), (0,)), ((), ()))
    back = lax.dot_general(w3[...], error, leading, preferred_element_type=F32)
    delta_2 = (back * slope_of(linear_2, sigmoid_2)).astype(jnp.bfloat16)
    back = lax.dot_general(w2[...], delta_2, leading, preferred_element_type=F32)
    delta_1 = (back * slope_of(linear_1, sigmoid_1)).astype(jnp.bfloat16)
    grad_1 = lax.dot_general(delta_1, inputs, contract, preferred_element_type=F32)
    grad_2 = lax.dot_general(delta_2, hidden_1, contract, preferred_element_type=F32)
    grad_3 = lax.dot_general(hidden_2, error, contract, preferred_element_type=F32)
    outputs = grad_3.shape[1]
    row = lax.broadcasted_iota(jnp.int32, (outputs, 128), 0)
    lane = lax.broadcasted_iota(jnp.int32, (outputs, 128), 1)
    grad_3 = jnp.dot(
        grad_3, jnp.where(lane == row + THIRD_AT, 1.0, 0.0), precision=EXACT, preferred_element_type=F32
    )
    parts = (grad_1[:, :128], grad_1[:, 128:], grad_2[:, :128], grad_2[:, 128:])
    for i, part in enumerate(parts):
        rows = slice(256 * i, 256 * i + 256)
        layers[rows, :] = part if first else layers_in[rows, :] + part
    third[...] = grad_3 if first else third_in[...] + grad_3


def share_kernel(arrived, copies):
    total = arrived[0:8, :]
    for i in range(1, arrived.shape[0] // 8):
        total = total + arrived[8 * i : 8 * i + 8, :]
    total = total + pltpu.roll(total, 4, 0)
    for i in range(copies.shape[0] // 8):
        copies[8 * i : 8 * i + 8, :] = total


def normal_kernel(whole, first, second):
    for at, out in ((0, first), (512, second)):
        rows = whole[at : at + 512, :]
        square = jnp.sum(jnp.sum(rows * rows, axis=0, keepdims=True), axis=1, keepdims=True)
        scale = lax.rsqrt(square / (out.shape[0] * out.shape[1]) + epsilon)
        out[:, :128] = rows[:256] * scale
        out[:, 128:] = rows[256:] * scale


def body(
    right_side,
    diagonal,
    element_features,
    sample_bank,
    target_bank,
    patch_index,
    w_first,
    w_second,
    w_third,
):
    devices = lax.axis_size(GX_GZ_GA)
    table = tables()
    layers = third = None
    count = patch_index.shape[0] // GROUPS
    for number in range(GROUPS):
        held = () if number == 0 else (layers, third)
        index = patch_index[count * number : count * number + count].reshape(1, count)
        layers, third = call(
            functools.partial(learn_kernel, number == 0), ((1024, 128), (devices, 128)), (),
            index, sample_bank, target_bank, w_first, w_second, w_third, *held,
            room=24, aliases={} if number == 0 else {6: 0, 7: 1},
        )
    slots = (devices, 4, 128)

    residual, precond, inverse, vector, *faces = call(
        start_kernel, (GRID,) * 4 + FACES, (), table, right_side, diagonal, element_features,
        w_first, w_second, w_third,
    )
    pressure = None
    weights, old_basis, old_images = None, [], []
    nothing = jnp.zeros((8, 128), F32)
    extra = {len(BLOCKS) - 2: third}
    for number, size in enumerate(BLOCKS):
        final = number + 1 == len(BLOCKS)
        old = len(old_basis)
        basis, images = [vector], []
        for j in range(size - 1):
            halo = exchange(faces)
            if final and j == size // 2:
                halo, whole = lax.optimization_barrier((halo, whole))
            image, vector, *faces = call(
                functools.partial(step_kernel, j == 0), (GRID, GRID) + FACES, HALO_SCRATCH,
                table, basis[-1], basis[max(j - 1, 0)], precond, inverse, *halo,
            )
            basis.append(vector)
            images.append(image)
        halo = exchange(faces)
        image, rows = call(
            functools.partial(last_kernel, size, old), (GRID, (devices, 128)), HALO_SCRATCH + ((128, 128),),
            table, precond, residual, extra.get(number, nothing), *halo, *basis, *images, *old_basis,
        )
        images.append(image)
        rows = all_rows(rows)
        if number == len(BLOCKS) - 2:
            arrived = all_rows(layers.reshape(slots)).reshape(1024, 128)
            copies = call(share_kernel, ((1024, 128),), (), arrived)[0]
            whole = all_rows(copies.reshape(slots)).reshape(1024, 128)
        given = [rows, table, residual, *basis, *images]
        shapes = [GRID, GRID]
        if old:
            given += [pressure, weights, *old_basis, *old_images]
        if final:
            shapes += [w_third.shape]
        else:
            given += [inverse]
            shapes += [GRID, *FACES, (64, 128), (8, 128)]
            if old:
                shapes += [GRID] * (2 * size)
        pressure, residual, *more = call(
            functools.partial(update_kernel, size, old, final), shapes, ((128, 128),), *given
        )
        if final:
            step_third = more[0]
        else:
            vector, faces, weights = more[0], more[1:7], more[7]
            if number == len(BLOCKS) - 2:
                extra[number + 1] = more[8]
            old_basis, old_images = basis, images
            if old:
                old_basis, old_images = more[9 : 9 + size], more[9 + size :]
    step_first, step_second = call(normal_kernel, (w_first.shape, w_second.shape), (), whole)
    return (pressure, residual, step_first, step_second, step_third)


def solution(mesh):
    finer = Mesh(
        mesh.devices.reshape(4, 2, 2, mesh.shape["gz"], mesh.shape["ga"]),
        GX_GZ_GA,
    )
    return jax.shard_map(
        body,
        mesh=finer,
        in_specs=(
            P(GX, "ga", "gz"),
            P(GX, "ga", "gz"),
            P(None, GX_GZ_GA),
            P(None, GX_GZ_GA),
            P(None, GX_GZ_GA),
            P(GX_GZ_GA),
            P(),
            P(),
            P(),
        ),
        out_specs=(P(GX, "ga", "gz"), P(GX, "ga", "gz"), P(), P(), P()),
        check_vma=False,
    )
```

```python
import functools

import jax
import jax.numpy as jnp
from jax import lax
from jax.experimental import pallas as pl
from jax.experimental.pallas import tpu as pltpu
from jax.sharding import Mesh
from jax.sharding import PartitionSpec as P

EL = 8
BLOCKS = (6, 6)
GROUPS = 4
GX = ("gx_0", "gx_1", "gx_2")
GX_GZ_GA = ("gx_0", "gx_1", "gx_2", "gz", "ga")

taps = (1.6, -0.2, 8.0 / 315.0, -1.0 / 560.0)
center = 3.0 * 205.0 / 72.0
epsilon = 1e-06
MIDDLE = 1.075
HALF = 0.925
THIRD_AT = 112
EXACT = lax.Precision.HIGHEST
F32 = jnp.float32
VMEM = pl.BlockSpec(memory_space=pltpu.VMEM)
HBM = pl.BlockSpec(memory_space=pltpu.HBM)


def after(kernel, count, waits, *refs):
    kernel(*refs[:count], *refs[count + waits :])


def call(kernel, out_shapes, scratch, *args, room=14, aliases={}, waits=()):
    scratch = [pltpu.VMEM(s, F32) for s in scratch]
    if waits:
        kernel = functools.partial(after, kernel, len(args), len(waits))
        args = (*args, *waits)
    return pl.pallas_call(
        kernel,
        out_shape=[jax.ShapeDtypeStruct(s, F32) for s in out_shapes],
        in_specs=[VMEM] * (len(args) - len(waits)) + [HBM] * len(waits),
        out_specs=[VMEM] * len(out_shapes),
        scratch_shapes=scratch,
        input_output_aliases=aliases,
        compiler_params=pltpu.CompilerParams(vmem_limit_bytes=room * 1024 * 1024),
    )(*args)


def pairs(count, odd):
    found = []
    for a in range(odd, count, 2):
        b = (a + 1) % count
        found += [(a, b), (b, a)]
    return found


def exchange(faces):
    xa, xb, ya, yb, za, zb = faces
    nx, ny, nz = lax.axis_size(GX), lax.axis_size("ga"), lax.axis_size("gz")
    return (
        lax.ppermute(xa, GX, pairs(nx, 0)),
        lax.ppermute(xb, GX, pairs(nx, 1)),
        lax.ppermute(ya, "ga", pairs(ny, 0)),
        lax.ppermute(yb, "ga", pairs(ny, 1)),
        lax.ppermute(za, "gz", pairs(nz, 0)),
        lax.ppermute(zb, "gz", pairs(nz, 1)),
    )


def tap_of(distance):
    distance = jnp.abs(distance)
    value = jnp.zeros(distance.shape, F32)
    for offset in range(1, 5):
        value = jnp.where(distance == offset, F32(taps[offset - 1]), value)
    return value


FLAGS, SELECT, SPREAD, BAND = 0, 8, 24, 40


def tables():
    rows = []
    even = {}
    inner = {}
    for name, axis in (("x", GX), ("y", "ga"), ("z", "gz")):
        index, count = lax.axis_index(axis), lax.axis_size(axis)
        even[name] = index % 2 == 0
        inner[name] = (index != 0) & (index != count - 1)
        rows += [even[name], inner[name]]
    rows += [even["x"], even["x"]]
    flags = jnp.broadcast_to(jnp.stack(rows).astype(F32)[:, None], (8, 128))
    row = lax.broadcasted_iota(jnp.int32, (16, 128), 0)
    lane = lax.broadcasted_iota(jnp.int32, (16, 128), 1)
    inside = row % 8
    upper = (row < 8) == even["z"]
    used = inside < 4
    select = jnp.where(used & (lane == inside + jnp.where(upper, 124, 0)), 1.0, 0.0)
    place = inside + jnp.where(upper, 128, -4)
    allowed = used & ((row < 8) | inner["z"])
    spread = jnp.where(allowed, tap_of(lane - place), 0.0)
    out = lax.broadcasted_iota(jnp.int32, (128, 128), 0)
    within = lax.broadcasted_iota(jnp.int32, (128, 128), 1)
    return jnp.concatenate([flags, select, spread, tap_of(out - within)], axis=0)


FACES = ((4, 32, 128), (4, 32, 128), (16, 4, 128), (16, 4, 128), (8, 512), (8, 512))
GRID = (16, 32, 128)


def write_faces(table, field, faces):
    xa, xb, ya, yb, za, zb = faces
    even_x = table[0:1, :] > 0.5
    even_y = table[2:3, :] > 0.5
    xa[...] = jnp.where(even_x, field[12:16], field[0:4])
    xb[...] = jnp.where(even_x, field[0:4], field[12:16])
    ya[...] = jnp.where(even_y, field[:, 28:32, :], field[:, 0:4, :])
    yb[...] = jnp.where(even_y, field[:, 0:4, :], field[:, 28:32, :])
    flat = field[...].reshape(512, 128)
    both = lax.dot_general(
        table[SELECT : SELECT + 16, :], flat, (((1,), (1,)), ((), ())),
        precision=EXACT, preferred_element_type=F32,
    )
    za[...] = both[0:8]
    zb[...] = both[8:16]


def image_planes(table, field, halo, xs, ys, zs, use):
    xa, xb, ya, yb, za, zb = halo
    even_x = table[0:1, :] > 0.5
    keep_x = table[1:2, :] > 0.5
    even_y = table[2:3, :] > 0.5
    keep_y = table[3:4, :] > 0.5
    outer = jnp.where(keep_x, xb[...], 0.0)
    xs[0:4] = jnp.where(even_x, outer, xa[...])
    xs[4:8] = jnp.where(even_x, xa[...], outer)
    outer = jnp.where(keep_y, yb[...], 0.0)
    ys[:, 4:8, :] = jnp.where(even_y, outer, ya[...])
    ys[:, 40:44, :] = jnp.where(even_y, ya[...], outer)
    ys[:, 8:40, :] = field[...]
    flat = field[...].reshape(512, 128)
    arrived = jnp.concatenate([za[...], zb[...]], axis=0)
    zs[...] = jnp.dot(
        flat, table[BAND : BAND + 128, :], precision=EXACT, preferred_element_type=F32
    ) + lax.dot_general(
        arrived, table[SPREAD : SPREAD + 16, :], (((0,), (0,)), ((), ())),
        precision=EXACT, preferred_element_type=F32,
    )

    def plane(i):
        if i < 0:
            return xs[i + 4]
        if i >= 16:
            return xs[i - 12]
        return field[i]

    for i in range(16):
        total = zs[32 * i : 32 * i + 32, :]
        for k in range(1, 5):
            along = (plane(i + k) + plane(i - k)) + (
                ys[i, 8 + k : 40 + k, :] + ys[i, 8 - k : 40 - k, :]
            )
            total = total + taps[k - 1] * along
        use(i, total)


HALO_SCRATCH = ((8, 32, 128), (16, 48, 128), (512, 128))


def start_kernel(table, right, diag, feats, w1, w2, w3, *rest):
    source, precond, inverse, basis = rest[:4]
    faces = rest[4:10]
    hidden = jnp.dot(w1[...], feats[...], preferred_element_type=F32)
    hidden = jax.nn.silu(hidden).astype(jnp.bfloat16)
    hidden = jnp.dot(w2[...], hidden, preferred_element_type=F32)
    hidden = jax.nn.silu(hidden).astype(jnp.bfloat16)
    stress = jnp.dot(w3[...], hidden, preferred_element_type=F32)
    trace = (stress[0:1] + stress[1:2] + stress[2:3]) / 3.0
    row = lax.broadcasted_iota(jnp.int32, (8, 128), 0)
    lane = lax.broadcasted_iota(jnp.int32, (8, 128), 1)
    apart = jnp.where(lane // 16 == row, trace, 0.0)
    element = lax.broadcasted_iota(jnp.int32, (128, 128), 0)
    node = lax.broadcasted_iota(jnp.int32, (128, 128), 1)
    widen = jnp.where(element % 16 == node // EL, 1.0, 0.0)
    wide = jnp.dot(apart, widen, precision=EXACT, preferred_element_type=F32)
    for i in range(16):
        for j in range(4):
            at = (i // EL) * 4 + j
            rows = slice(EL * j, EL * j + EL)
            value = right[i, rows, :] + wide[at : at + 1, :]
            weight = diag[i, rows, :] + center
            source[i, rows, :] = value
            precond[i, rows, :] = weight
            inverted = 1.0 / weight
            inverse[i, rows, :] = inverted
            basis[i, rows, :] = value * inverted
    write_faces(table, basis, faces)


def step_kernel(first, table, field, before, precond, inverse, *rest):
    halo, rest = rest[:6], rest[6:]
    image, after = rest[:2]
    faces, scratch = rest[2:8], rest[8:]

    def use(i, total):
        value = field[i]
        image[i] = precond[i] * value - total
        if first:
            after[i] = ((1.0 - MIDDLE) * value - total * inverse[i]) * (1.0 / HALF)
        else:
            after[i] = ((1.0 - MIDDLE) * value - total * inverse[i]) * (2.0 / HALF) - before[i]

    image_planes(table, field, halo, *scratch, use)
    write_faces(table, after, faces)


def products(size, old):
    wanted = [(("t", i), ("q", j)) for i in range(size) for j in range(i, size)]
    wanted += [(("t", i), ("r", 0)) for i in range(size)]
    groups = [wanted]
    if old:
        for i0 in range(0, old, 4):
            some = range(i0, min(old, i0 + 4))
            groups.append([(("p", i), ("q", j)) for i in some for j in range(size)] + [(("p", i), ("r", 0)) for i in some])
    return groups


def last_kernel(size, old, table, precond, residual, extra, *rest):
    halo, rest = rest[:6], rest[6:]
    basis, rest = rest[:size], rest[size:]
    images, rest = rest[: size - 1], rest[size - 1 :]
    olds, rest = rest[:old], rest[old:]
    image, row = rest[:2]
    scratch, sums = rest[2:5], rest[5]
    field = basis[-1]

    def use(i, total):
        image[i] = precond[i] * field[i] - total

    image_planes(table, field, halo, *scratch, use)
    refs = {("r", 0): residual}
    for j in range(size):
        refs["t", j] = basis[j]
        refs["q", j] = images[j] if j < size - 1 else image
    for j in range(old):
        refs["p", j] = olds[j]
    sums[...] = jnp.zeros(sums.shape, F32)
    at = 0
    for group in products(size, old):
        names = sorted({name for pair in group for name in pair})

        def add(i, totals, names=names, group=group):
            for part in range(4):
                value = {n: refs[n][i, 8 * part : 8 * part + 8, :] for n in names}
                totals = tuple(
                    total + value[a] * value[b] for total, (a, b) in zip(totals, group)
                )
            return totals

        totals = lax.fori_loop(0, 16, add, (jnp.zeros((8, 128), F32),) * len(group))
        for total in totals:
            sums[at : at + 1, :] = jnp.sum(total, axis=0, keepdims=True)
            at += 1
    packed = lax.dot_general(
        jnp.ones((8, 128), F32), sums[...], (((1,), (1,)), ((), ())),
        precision=EXACT, preferred_element_type=F32,
    )
    shared = extra.shape[0] == 8
    for i in range(row.shape[0] // 8):
        rows = slice(8 * i, 8 * i + 8)
        row[rows, :] = packed + (extra[...] if shared else extra[rows, :])


def factor(matrix, size):
    low, scaled, inverse = {}, {}, []
    for j in range(size):
        pivot = matrix[j][j]
        for k in range(j):
            pivot = pivot - low[j, k] * scaled[j, k]
        inverse.append(1.0 / pivot)
        for i in range(j + 1, size):
            value = matrix[i][j]
            for k in range(j):
                value = value - scaled[i, k] * low[j, k]
            scaled[i, j] = value
            low[i, j] = value * inverse[j]
    return low, inverse


def solve(factors, size, right):
    low, inverse = factors
    found = []
    for i in range(size):
        value = right[i]
        for k in range(i):
            value = value - low[i, k] * found[k]
        found.append(value)
    found = [a * b for a, b in zip(found, inverse)]
    for i in reversed(range(size)):
        for k in range(i + 1, size):
            found[i] = found[i] - low[k, i] * found[k]
    return found


def update_kernel(size, old, final, *rest):
    gathered, table, residual, rest = rest[0], rest[1], rest[2], rest[3:]
    basis, rest = rest[:size], rest[size:]
    images, rest = rest[:size], rest[size:]
    if old:
        pressure, weights, rest = rest[0], rest[1], rest[2:]
        old_basis, rest = rest[:old], rest[old:]
        old_images, rest = rest[:old], rest[old:]
    if not final:
        inverse, rest = rest[0], rest[1:]
    new_pressure, new_residual = rest[:2]
    rest = rest[2:]
    if final:
        third, rest = rest[0], rest[1:]
    else:
        after, faces, new_weights, share, rest = rest[0], rest[1:7], rest[7], rest[8], rest[9:]
        if old:
            new_basis, rest = rest[:size], rest[size:]
            new_images, rest = rest[:size], rest[size:]
    splats = rest[0]
    totals = jnp.sum(gathered[...], axis=0, keepdims=True)
    row = lax.broadcasted_iota(jnp.int32, (128, 128), 0)
    lane = lax.broadcasted_iota(jnp.int32, (128, 128), 1)
    splats[...] = jnp.dot(
        jnp.where((row == lane) & (lane < THIRD_AT), totals, 0.0), jnp.ones((128, 128), F32),
        precision=EXACT, preferred_element_type=F32,
    )
    if final:
        at_row = lax.broadcasted_iota(jnp.int32, (8, 128), 0)
        at_lane = lax.broadcasted_iota(jnp.int32, (8, 128), 1)
        taken = lax.dot_general(
            jnp.where((at_lane == at_row + THIRD_AT) & (at_row < third.shape[0]), 1.0, 0.0), gathered[...],
            (((1,), (1,)), ((), ())), precision=EXACT, preferred_element_type=F32,
        )
        square = jnp.sum(jnp.sum(taken * taken, axis=0, keepdims=True), axis=1, keepdims=True)
        taken = taken * lax.rsqrt(square / (third.shape[0] * third.shape[1]) + epsilon)
        third[...] = taken[: third.shape[0]]
    else:
        kept = jnp.where(lane[0:8] < THIRD_AT, 0.0, totals)
        share[...] = kept
    value = {}
    at = 0
    for group in products(size, old):
        for a, b in group:
            value[a, b] = splats[at : at + 1, :]
            at += 1
    gram = [[value[("t", min(i, j)), ("q", max(i, j))] for j in range(size)] for i in range(size)]
    right = [value[("t", i), ("r", 0)] for i in range(size)]
    mix = None
    if old:
        cross = [[value[("p", i), ("q", j)] for j in range(size)] for i in range(old)]
        held = [[weights[i * old + j : i * old + j + 1, :] for j in range(old)] for i in range(old)]
        factors = factor(held, old)
        columns = [solve(factors, old, [-cross[i][j] for i in range(old)]) for j in range(size)]
        behind = [value[("p", i), ("r", 0)] for i in range(old)]
        for j in range(size):
            for k in range(old):
                right[j] = right[j] + columns[j][k] * behind[k]
        behind = solve(factors, old, behind)
        for i in range(size):
            for j in range(i, size):
                for k in range(old):
                    gram[i][j] = gram[i][j] + cross[k][i] * columns[j][k]
                gram[j][i] = gram[i][j]
        mix = [[jnp.broadcast_to(v, (8, 128)) for v in column] for column in columns]
    step = solve(factor(gram, size), size, right)
    if not final:
        new_weights[...] = jnp.zeros(new_weights.shape, F32)
        for i in range(size):
            for j in range(size):
                new_weights[i * size + j : i * size + j + 1, :] = gram[i][j]
    if old:
        carried = []
        for i in range(old):
            total = behind[i]
            if final:
                for j in range(size):
                    total = total + step[j] * columns[j][i]
            carried.append(jnp.broadcast_to(total, (8, 128)))
    step = [jnp.broadcast_to(v, (8, 128)) for v in step]

    def tile(i, part):
        rows = slice(8 * part, 8 * part + 8)
        vectors = [ref[i, rows, :] for ref in basis]
        duals = [ref[i, rows, :] for ref in images]
        if old and not final:
            held_v = [ref[i, rows, :] for ref in old_basis]
            held_d = [ref[i, rows, :] for ref in old_images]
            for j in range(size):
                for k in range(old):
                    vectors[j] = vectors[j] + mix[j][k] * held_v[k]
                    duals[j] = duals[j] + mix[j][k] * held_d[k]
                new_basis[j][i, rows, :] = vectors[j]
                new_images[j][i, rows, :] = duals[j]
        gain = step[0] * vectors[0]
        loss = step[0] * duals[0]
        for j in range(1, size):
            gain = gain + step[j] * vectors[j]
            loss = loss + step[j] * duals[j]
        if old:
            for k in range(old):
                gain = gain + carried[k] * old_basis[k][i, rows, :]
                loss = loss + carried[k] * old_images[k][i, rows, :]
        if old:
            gain = pressure[i, rows, :] + gain
        left = residual[i, rows, :] - loss
        new_pressure[i, rows, :] = gain
        new_residual[i, rows, :] = left
        if not final:
            after[i, rows, :] = left * inverse[i, rows, :]

    def planes(i, nothing):
        for part in range(4):
            tile(i, part)
        return nothing

    lax.fori_loop(0, 16, planes, 0)
    if not final:
        write_faces(table, after, faces)


def all_rows(rows):
    return lax.all_to_all(rows, GX_GZ_GA, split_axis=0, concat_axis=0, tiled=True)


def slope_of(linear, sigmoid):
    return sigmoid * (1.0 + linear * (1.0 - sigmoid))


def learn_kernel(first, index, bank, target, w1, w2, w3, *rest):
    if not first:
        layers_in, third_in, rest = rest[0], rest[1], rest[2:]
    layers, third = rest
    group = index.shape[1]
    column = lax.broadcasted_iota(jnp.int32, (bank.shape[1], group), 0)
    chosen = jnp.where(column == index[...], 1.0, 0.0).astype(jnp.bfloat16)
    inputs = jnp.dot(bank[...], chosen, preferred_element_type=F32).astype(jnp.bfloat16)
    wanted = jnp.dot(target[...], chosen, preferred_element_type=F32)
    linear_1 = jnp.dot(w1[...], inputs, preferred_element_type=F32)
    sigmoid_1 = 1.0 / (1.0 + jnp.exp(-linear_1))
    hidden_1 = (linear_1 * sigmoid_1).astype(jnp.bfloat16)
    linear_2 = jnp.dot(w2[...], hidden_1, preferred_element_type=F32)
    sigmoid_2 = 1.0 / (1.0 + jnp.exp(-linear_2))
    hidden_2 = (linear_2 * sigmoid_2).astype(jnp.bfloat16)
    stress = jnp.dot(w3[...], hidden_2, preferred_element_type=F32)
    error = (stress - wanted).astype(jnp.bfloat16)
    contract = (((1,), (1,)), ((), ()))
    leading = (((0,), (0,)), ((), ()))
    back = lax.dot_general(w3[...], error, leading, preferred_element_type=F32)
    delta_2 = (back * slope_of(linear_2, sigmoid_2)).astype(jnp.bfloat16)
    back = lax.dot_general(w2[...], delta_2, leading, preferred_element_type=F32)
    delta_1 = (back * slope_of(linear_1, sigmoid_1)).astype(jnp.bfloat16)
    grad_1 = lax.dot_general(delta_1, inputs, contract, preferred_element_type=F32)
    grad_2 = lax.dot_general(delta_2, hidden_1, contract, preferred_element_type=F32)
    grad_3 = lax.dot_general(hidden_2, error, contract, preferred_element_type=F32)
    outputs = grad_3.shape[1]
    row = lax.broadcasted_iota(jnp.int32, (outputs, 128), 0)
    lane = lax.broadcasted_iota(jnp.int32, (outputs, 128), 1)
    grad_3 = jnp.dot(
        grad_3, jnp.where(lane == row + THIRD_AT, 1.0, 0.0), precision=EXACT, preferred_element_type=F32
    )
    parts = (grad_1[:, :128], grad_1[:, 128:], grad_2[:, :128], grad_2[:, 128:])
    for i, part in enumerate(parts):
        rows = slice(256 * i, 256 * i + 256)
        layers[rows, :] = part if first else layers_in[rows, :] + part
    third[...] = grad_3 if first else third_in[...] + grad_3


def share_kernel(arrived, copies):
    total = arrived[0:8, :]
    for i in range(1, arrived.shape[0] // 8):
        total = total + arrived[8 * i : 8 * i + 8, :]
    total = total + pltpu.roll(total, 4, 0)
    for i in range(copies.shape[0] // 8):
        copies[8 * i : 8 * i + 8, :] = total


def normal_kernel(whole, first, second):
    for at, out in ((0, first), (512, second)):
        rows = whole[at : at + 512, :]
        square = jnp.sum(jnp.sum(rows * rows, axis=0, keepdims=True), axis=1, keepdims=True)
        scale = lax.rsqrt(square / (out.shape[0] * out.shape[1]) + epsilon)
        out[:, :128] = rows[:256] * scale
        out[:, 128:] = rows[256:] * scale


def body(
    right_side,
    diagonal,
    element_features,
    sample_bank,
    target_bank,
    patch_index,
    w_first,
    w_second,
    w_third,
):
    devices = lax.axis_size(GX_GZ_GA)
    table = tables()
    layers = third = None
    count = patch_index.shape[0] // GROUPS
    for number in range(GROUPS):
        held = () if number == 0 else (layers, third)
        index = patch_index[count * number : count * number + count].reshape(1, count)
        layers, third = call(
            functools.partial(learn_kernel, number == 0), ((1024, 128), (devices, 128)), (),
            index, sample_bank, target_bank, w_first, w_second, w_third, *held,
            room=24, aliases={} if number == 0 else {6: 0, 7: 1},
        )
    slots = (devices, 4, 128)
    arrived = all_rows(layers.reshape(slots)).reshape(1024, 128)
    copies = call(share_kernel, ((1024, 128),), (), arrived)[0]
    whole = all_rows(copies.reshape(slots)).reshape(1024, 128)
    step_first, step_second = call(normal_kernel, (w_first.shape, w_second.shape), (), whole)
    order = {(0, 0): (copies,), (0, 2): (step_first,)}

    residual, precond, inverse, vector, *faces = call(
        start_kernel, (GRID,) * 4 + FACES, (), table, right_side, diagonal, element_features,
        w_first, w_second, w_third,
    )
    pressure = None
    weights, old_basis, old_images = None, [], []
    nothing = jnp.zeros((8, 128), F32)
    extra = {len(BLOCKS) - 2: third}
    for number, size in enumerate(BLOCKS):
        final = number + 1 == len(BLOCKS)
        old = len(old_basis)
        basis, images = [vector], []
        for j in range(size - 1):
            halo = exchange(faces)
            image, vector, *faces = call(
                functools.partial(step_kernel, j == 0), (GRID, GRID) + FACES, HALO_SCRATCH,
                table, basis[-1], basis[max(j - 1, 0)], precond, inverse, *halo,
                waits=order.get((number, j), ()),
            )
            basis.append(vector)
            images.append(image)
        halo = exchange(faces)
        image, rows = call(
            functools.partial(last_kernel, size, old), (GRID, (devices, 128)), HALO_SCRATCH + ((128, 128),),
            table, precond, residual, extra.get(number, nothing), *halo, *basis, *images, *old_basis,
            waits=(step_first, step_second) if number == 0 else (),
        )
        images.append(image)
        rows = all_rows(rows)
        given = [rows, table, residual, *basis, *images]
        shapes = [GRID, GRID]
        if old:
            given += [pressure, weights, *old_basis, *old_images]
        if final:
            shapes += [w_third.shape]
        else:
            given += [inverse]
            shapes += [GRID, *FACES, (64, 128), (8, 128)]
            if old:
                shapes += [GRID] * (2 * size)
        pressure, residual, *more = call(
            functools.partial(update_kernel, size, old, final), shapes, ((128, 128),), *given
        )
        if final:
            step_third = more[0]
        else:
            vector, faces, weights = more[0], more[1:7], more[7]
            if number == len(BLOCKS) - 2:
                extra[number + 1] = more[8]
            old_basis, old_images = basis, images
            if old:
                old_basis, old_images = more[9 : 9 + size], more[9 + size :]
    return (pressure, residual, step_first, step_second, step_third)


def solution(mesh):
    finer = Mesh(
        mesh.devices.reshape(4, 2, 2, mesh.shape["gz"], mesh.shape["ga"]),
        GX_GZ_GA,
    )
    return jax.shard_map(
        body,
        mesh=finer,
        in_specs=(
            P(GX, "ga", "gz"),
            P(GX, "ga", "gz"),
            P(None, GX_GZ_GA),
            P(None, GX_GZ_GA),
            P(None, GX_GZ_GA),
            P(GX_GZ_GA),
            P(),
            P(),
            P(),
        ),
        out_specs=(P(GX, "ga", "gz"), P(GX, "ga", "gz"), P(), P(), P()),
        check_vma=False,
    )
```

```python
import functools

import jax
import jax.numpy as jnp
from jax import lax
from jax.experimental import pallas as pl
from jax.experimental.pallas import tpu as pltpu
from jax.sharding import Mesh
from jax.sharding import PartitionSpec as P

EL = 8
BLOCKS = (6, 6)
GROUPS = 4
GX = ("gx_0", "gx_1", "gx_2")
GX_GZ_GA = ("gx_0", "gx_1", "gx_2", "gz", "ga")

taps = (1.6, -0.2, 8.0 / 315.0, -1.0 / 560.0)
center = 3.0 * 205.0 / 72.0
epsilon = 1e-06
MIDDLE = 1.075
HALF = 0.925
THIRD_AT = 112
EXACT = lax.Precision.HIGHEST
F32 = jnp.float32
VMEM = pl.BlockSpec(memory_space=pltpu.VMEM)
TOKEN = (8, 128)


def after(kernel, count, waits, token, *refs):
    kernel(*refs[:count], *refs[count + waits : token], *refs[token + 1 :])
    refs[token][...] = jnp.zeros(TOKEN, F32)


def call(kernel, out_shapes, scratch, *args, room=14, aliases={}, waits=()):
    scratch = [pltpu.VMEM(s, F32) for s in scratch]
    out_shapes = (*out_shapes, TOKEN)
    count = len(args)
    args = (*args, *waits)
    kernel = functools.partial(after, kernel, count, len(waits), len(args) + len(out_shapes) - 1)
    return pl.pallas_call(
        kernel,
        out_shape=[jax.ShapeDtypeStruct(s, F32) for s in out_shapes],
        in_specs=[VMEM] * len(args),
        out_specs=[VMEM] * len(out_shapes),
        scratch_shapes=scratch,
        input_output_aliases=aliases,
        compiler_params=pltpu.CompilerParams(vmem_limit_bytes=room * 1024 * 1024),
    )(*args)


def pairs(count, odd):
    found = []
    for a in range(odd, count, 2):
        b = (a + 1) % count
        found += [(a, b), (b, a)]
    return found


def exchange(faces):
    xa, xb, ya, yb, za, zb = faces
    nx, ny, nz = lax.axis_size(GX), lax.axis_size("ga"), lax.axis_size("gz")
    return (
        lax.ppermute(xa, GX, pairs(nx, 0)),
        lax.ppermute(xb, GX, pairs(nx, 1)),
        lax.ppermute(ya, "ga", pairs(ny, 0)),
        lax.ppermute(yb, "ga", pairs(ny, 1)),
        lax.ppermute(za, "gz", pairs(nz, 0)),
        lax.ppermute(zb, "gz", pairs(nz, 1)),
    )


def tap_of(distance):
    distance = jnp.abs(distance)
    value = jnp.zeros(distance.shape, F32)
    for offset in range(1, 5):
        value = jnp.where(distance == offset, F32(taps[offset - 1]), value)
    return value


FLAGS, SELECT, SPREAD, BAND = 0, 8, 24, 40


def tables():
    rows = []
    even = {}
    inner = {}
    for name, axis in (("x", GX), ("y", "ga"), ("z", "gz")):
        index, count = lax.axis_index(axis), lax.axis_size(axis)
        even[name] = index % 2 == 0
        inner[name] = (index != 0) & (index != count - 1)
        rows += [even[name], inner[name]]
    rows += [even["x"], even["x"]]
    flags = jnp.broadcast_to(jnp.stack(rows).astype(F32)[:, None], (8, 128))
    row = lax.broadcasted_iota(jnp.int32, (16, 128), 0)
    lane = lax.broadcasted_iota(jnp.int32, (16, 128), 1)
    inside = row % 8
    upper = (row < 8) == even["z"]
    used = inside < 4
    select = jnp.where(used & (lane == inside + jnp.where(upper, 124, 0)), 1.0, 0.0)
    place = inside + jnp.where(upper, 128, -4)
    allowed = used & ((row < 8) | inner["z"])
    spread = jnp.where(allowed, tap_of(lane - place), 0.0)
    out = lax.broadcasted_iota(jnp.int32, (128, 128), 0)
    within = lax.broadcasted_iota(jnp.int32, (128, 128), 1)
    return jnp.concatenate([flags, select, spread, tap_of(out - within)], axis=0)


FACES = ((4, 32, 128), (4, 32, 128), (16, 4, 128), (16, 4, 128), (8, 512), (8, 512))
GRID = (16, 32, 128)


def write_faces(table, field, faces):
    xa, xb, ya, yb, za, zb = faces
    even_x = table[0:1, :] > 0.5
    even_y = table[2:3, :] > 0.5
    xa[...] = jnp.where(even_x, field[12:16], field[0:4])
    xb[...] = jnp.where(even_x, field[0:4], field[12:16])
    ya[...] = jnp.where(even_y, field[:, 28:32, :], field[:, 0:4, :])
    yb[...] = jnp.where(even_y, field[:, 0:4, :], field[:, 28:32, :])
    flat = field[...].reshape(512, 128)
    both = lax.dot_general(
        table[SELECT : SELECT + 16, :], flat, (((1,), (1,)), ((), ())),
        precision=EXACT, preferred_element_type=F32,
    )
    za[...] = both[0:8]
    zb[...] = both[8:16]


def image_planes(table, field, halo, xs, ys, zs, use):
    xa, xb, ya, yb, za, zb = halo
    even_x = table[0:1, :] > 0.5
    keep_x = table[1:2, :] > 0.5
    even_y = table[2:3, :] > 0.5
    keep_y = table[3:4, :] > 0.5
    outer = jnp.where(keep_x, xb[...], 0.0)
    xs[0:4] = jnp.where(even_x, outer, xa[...])
    xs[4:8] = jnp.where(even_x, xa[...], outer)
    outer = jnp.where(keep_y, yb[...], 0.0)
    ys[:, 4:8, :] = jnp.where(even_y, outer, ya[...])
    ys[:, 40:44, :] = jnp.where(even_y, ya[...], outer)
    ys[:, 8:40, :] = field[...]
    flat = field[...].reshape(512, 128)
    arrived = jnp.concatenate([za[...], zb[...]], axis=0)
    zs[...] = jnp.dot(
        flat, table[BAND : BAND + 128, :], precision=EXACT, preferred_element_type=F32
    ) + lax.dot_general(
        arrived, table[SPREAD : SPREAD + 16, :], (((0,), (0,)), ((), ())),
        precision=EXACT, preferred_element_type=F32,
    )

    def plane(i):
        if i < 0:
            return xs[i + 4]
        if i >= 16:
            return xs[i - 12]
        return field[i]

    for i in range(16):
        total = zs[32 * i : 32 * i + 32, :]
        for k in range(1, 5):
            along = (plane(i + k) + plane(i - k)) + (
                ys[i, 8 + k : 40 + k, :] + ys[i, 8 - k : 40 - k, :]
            )
            total = total + taps[k - 1] * along
        use(i, total)


HALO_SCRATCH = ((8, 32, 128), (16, 48, 128), (512, 128))


def start_kernel(table, right, diag, feats, w1, w2, w3, *rest):
    source, precond, inverse, basis = rest[:4]
    faces = rest[4:10]
    hidden = jnp.dot(w1[...], feats[...], preferred_element_type=F32)
    hidden = jax.nn.silu(hidden).astype(jnp.bfloat16)
    hidden = jnp.dot(w2[...], hidden, preferred_element_type=F32)
    hidden = jax.nn.silu(hidden).astype(jnp.bfloat16)
    stress = jnp.dot(w3[...], hidden, preferred_element_type=F32)
    trace = (stress[0:1] + stress[1:2] + stress[2:3]) / 3.0
    row = lax.broadcasted_iota(jnp.int32, (8, 128), 0)
    lane = lax.broadcasted_iota(jnp.int32, (8, 128), 1)
    apart = jnp.where(lane // 16 == row, trace, 0.0)
    element = lax.broadcasted_iota(jnp.int32, (128, 128), 0)
    node = lax.broadcasted_iota(jnp.int32, (128, 128), 1)
    widen = jnp.where(element % 16 == node // EL, 1.0, 0.0)
    wide = jnp.dot(apart, widen, precision=EXACT, preferred_element_type=F32)
    for i in range(16):
        for j in range(4):
            at = (i // EL) * 4 + j
            rows = slice(EL * j, EL * j + EL)
            value = right[i, rows, :] + wide[at : at + 1, :]
            weight = diag[i, rows, :] + center
            source[i, rows, :] = value
            precond[i, rows, :] = weight
            inverted = 1.0 / weight
            inverse[i, rows, :] = inverted
            basis[i, rows, :] = value * inverted
    write_faces(table, basis, faces)


def step_kernel(first, table, field, before, precond, inverse, *rest):
    halo, rest = rest[:6], rest[6:]
    image, after = rest[:2]
    faces, scratch = rest[2:8], rest[8:]

    def use(i, total):
        value = field[i]
        image[i] = precond[i] * value - total
        if first:
            after[i] = ((1.0 - MIDDLE) * value - total * inverse[i]) * (1.0 / HALF)
        else:
            after[i] = ((1.0 - MIDDLE) * value - total * inverse[i]) * (2.0 / HALF) - before[i]

    image_planes(table, field, halo, *scratch, use)
    write_faces(table, after, faces)


def products(size, old):
    wanted = [(("t", i), ("q", j)) for i in range(size) for j in range(i, size)]
    wanted += [(("t", i), ("r", 0)) for i in range(size)]
    groups = [wanted]
    if old:
        for i0 in range(0, old, 4):
            some = range(i0, min(old, i0 + 4))
            groups.append([(("p", i), ("q", j)) for i in some for j in range(size)] + [(("p", i), ("r", 0)) for i in some])
    return groups


def last_kernel(size, old, table, precond, residual, extra, *rest):
    halo, rest = rest[:6], rest[6:]
    basis, rest = rest[:size], rest[size:]
    images, rest = rest[: size - 1], rest[size - 1 :]
    olds, rest = rest[:old], rest[old:]
    image, row = rest[:2]
    scratch, sums = rest[2:5], rest[5]
    field = basis[-1]

    def use(i, total):
        image[i] = precond[i] * field[i] - total

    image_planes(table, field, halo, *scratch, use)
    refs = {("r", 0): residual}
    for j in range(size):
        refs["t", j] = basis[j]
        refs["q", j] = images[j] if j < size - 1 else image
    for j in range(old):
        refs["p", j] = olds[j]
    sums[...] = jnp.zeros(sums.shape, F32)
    at = 0
    for group in products(size, old):
        names = sorted({name for pair in group for name in pair})

        def add(i, totals, names=names, group=group):
            for part in range(4):
                value = {n: refs[n][i, 8 * part : 8 * part + 8, :] for n in names}
                totals = tuple(
                    total + value[a] * value[b] for total, (a, b) in zip(totals, group)
                )
            return totals

        totals = lax.fori_loop(0, 16, add, (jnp.zeros((8, 128), F32),) * len(group))
        for total in totals:
            sums[at : at + 1, :] = jnp.sum(total, axis=0, keepdims=True)
            at += 1
    packed = lax.dot_general(
        jnp.ones((8, 128), F32), sums[...], (((1,), (1,)), ((), ())),
        precision=EXACT, preferred_element_type=F32,
    )
    shared = extra.shape[0] == 8
    for i in range(row.shape[0] // 8):
        rows = slice(8 * i, 8 * i + 8)
        row[rows, :] = packed + (extra[...] if shared else extra[rows, :])


def factor(matrix, size):
    low, scaled, inverse = {}, {}, []
    for j in range(size):
        pivot = matrix[j][j]
        for k in range(j):
            pivot = pivot - low[j, k] * scaled[j, k]
        inverse.append(1.0 / pivot)
        for i in range(j + 1, size):
            value = matrix[i][j]
            for k in range(j):
                value = value - scaled[i, k] * low[j, k]
            scaled[i, j] = value
            low[i, j] = value * inverse[j]
    return low, inverse


def solve(factors, size, right):
    low, inverse = factors
    found = []
    for i in range(size):
        value = right[i]
        for k in range(i):
            value = value - low[i, k] * found[k]
        found.append(value)
    found = [a * b for a, b in zip(found, inverse)]
    for i in reversed(range(size)):
        for k in range(i + 1, size):
            found[i] = found[i] - low[k, i] * found[k]
    return found


def update_kernel(size, old, final, *rest):
    gathered, table, residual, rest = rest[0], rest[1], rest[2], rest[3:]
    basis, rest = rest[:size], rest[size:]
    images, rest = rest[:size], rest[size:]
    if old:
        pressure, weights, rest = rest[0], rest[1], rest[2:]
        old_basis, rest = rest[:old], rest[old:]
        old_images, rest = rest[:old], rest[old:]
    if not final:
        inverse, rest = rest[0], rest[1:]
    new_pressure, new_residual = rest[:2]
    rest = rest[2:]
    if final:
        third, rest = rest[0], rest[1:]
    else:
        after, faces, new_weights, share, rest = rest[0], rest[1:7], rest[7], rest[8], rest[9:]
        if old:
            new_basis, rest = rest[:size], rest[size:]
            new_images, rest = rest[:size], rest[size:]
    splats = rest[0]
    totals = jnp.sum(gathered[...], axis=0, keepdims=True)
    row = lax.broadcasted_iota(jnp.int32, (128, 128), 0)
    lane = lax.broadcasted_iota(jnp.int32, (128, 128), 1)
    splats[...] = jnp.dot(
        jnp.where((row == lane) & (lane < THIRD_AT), totals, 0.0), jnp.ones((128, 128), F32),
        precision=EXACT, preferred_element_type=F32,
    )
    if final:
        at_row = lax.broadcasted_iota(jnp.int32, (8, 128), 0)
        at_lane = lax.broadcasted_iota(jnp.int32, (8, 128), 1)
        taken = lax.dot_general(
            jnp.where((at_lane == at_row + THIRD_AT) & (at_row < third.shape[0]), 1.0, 0.0), gathered[...],
            (((1,), (1,)), ((), ())), precision=EXACT, preferred_element_type=F32,
        )
        square = jnp.sum(jnp.sum(taken * taken, axis=0, keepdims=True), axis=1, keepdims=True)
        taken = taken * lax.rsqrt(square / (third.shape[0] * third.shape[1]) + epsilon)
        third[...] = taken[: third.shape[0]]
    else:
        kept = jnp.where(lane[0:8] < THIRD_AT, 0.0, totals)
        share[...] = kept
    value = {}
    at = 0
    for group in products(size, old):
        for a, b in group:
            value[a, b] = splats[at : at + 1, :]
            at += 1
    gram = [[value[("t", min(i, j)), ("q", max(i, j))] for j in range(size)] for i in range(size)]
    right = [value[("t", i), ("r", 0)] for i in range(size)]
    mix = None
    if old:
        cross = [[value[("p", i), ("q", j)] for j in range(size)] for i in range(old)]
        held = [[weights[i * old + j : i * old + j + 1, :] for j in range(old)] for i in range(old)]
        factors = factor(held, old)
        columns = [solve(factors, old, [-cross[i][j] for i in range(old)]) for j in range(size)]
        behind = [value[("p", i), ("r", 0)] for i in range(old)]
        for j in range(size):
            for k in range(old):
                right[j] = right[j] + columns[j][k] * behind[k]
        behind = solve(factors, old, behind)
        for i in range(size):
            for j in range(i, size):
                for k in range(old):
                    gram[i][j] = gram[i][j] + cross[k][i] * columns[j][k]
                gram[j][i] = gram[i][j]
        mix = [[jnp.broadcast_to(v, (8, 128)) for v in column] for column in columns]
    step = solve(factor(gram, size), size, right)
    if not final:
        new_weights[...] = jnp.zeros(new_weights.shape, F32)
        for i in range(size):
            for j in range(size):
                new_weights[i * size + j : i * size + j + 1, :] = gram[i][j]
    if old:
        carried = []
        for i in range(old):
            total = behind[i]
            if final:
                for j in range(size):
                    total = total + step[j] * columns[j][i]
            carried.append(jnp.broadcast_to(total, (8, 128)))
    step = [jnp.broadcast_to(v, (8, 128)) for v in step]

    def tile(i, part):
        rows = slice(8 * part, 8 * part + 8)
        vectors = [ref[i, rows, :] for ref in basis]
        duals = [ref[i, rows, :] for ref in images]
        if old and not final:
            held_v = [ref[i, rows, :] for ref in old_basis]
            held_d = [ref[i, rows, :] for ref in old_images]
            for j in range(size):
                for k in range(old):
                    vectors[j] = vectors[j] + mix[j][k] * held_v[k]
                    duals[j] = duals[j] + mix[j][k] * held_d[k]
                new_basis[j][i, rows, :] = vectors[j]
                new_images[j][i, rows, :] = duals[j]
        gain = step[0] * vectors[0]
        loss = step[0] * duals[0]
        for j in range(1, size):
            gain = gain + step[j] * vectors[j]
            loss = loss + step[j] * duals[j]
        if old:
            for k in range(old):
                gain = gain + carried[k] * old_basis[k][i, rows, :]
                loss = loss + carried[k] * old_images[k][i, rows, :]
        if old:
            gain = pressure[i, rows, :] + gain
        left = residual[i, rows, :] - loss
        new_pressure[i, rows, :] = gain
        new_residual[i, rows, :] = left
        if not final:
            after[i, rows, :] = left * inverse[i, rows, :]

    def planes(i, nothing):
        for part in range(4):
            tile(i, part)
        return nothing

    lax.fori_loop(0, 16, planes, 0)
    if not final:
        write_faces(table, after, faces)


def all_rows(rows):
    return lax.all_to_all(rows, GX_GZ_GA, split_axis=0, concat_axis=0, tiled=True)


def slope_of(linear, sigmoid):
    return sigmoid * (1.0 + linear * (1.0 - sigmoid))


def learn_kernel(first, index, bank, target, w1, w2, w3, *rest):
    if not first:
        layers_in, third_in, rest = rest[0], rest[1], rest[2:]
    layers, third = rest
    group = index.shape[1]
    column = lax.broadcasted_iota(jnp.int32, (bank.shape[1], group), 0)
    chosen = jnp.where(column == index[...], 1.0, 0.0).astype(jnp.bfloat16)
    inputs = jnp.dot(bank[...], chosen, preferred_element_type=F32).astype(jnp.bfloat16)
    wanted = jnp.dot(target[...], chosen, preferred_element_type=F32)
    linear_1 = jnp.dot(w1[...], inputs, preferred_element_type=F32)
    sigmoid_1 = 1.0 / (1.0 + jnp.exp(-linear_1))
    hidden_1 = (linear_1 * sigmoid_1).astype(jnp.bfloat16)
    linear_2 = jnp.dot(w2[...], hidden_1, preferred_element_type=F32)
    sigmoid_2 = 1.0 / (1.0 + jnp.exp(-linear_2))
    hidden_2 = (linear_2 * sigmoid_2).astype(jnp.bfloat16)
    stress = jnp.dot(w3[...], hidden_2, preferred_element_type=F32)
    error = (stress - wanted).astype(jnp.bfloat16)
    contract = (((1,), (1,)), ((), ()))
    leading = (((0,), (0,)), ((), ()))
    back = lax.dot_general(w3[...], error, leading, preferred_element_type=F32)
    delta_2 = (back * slope_of(linear_2, sigmoid_2)).astype(jnp.bfloat16)
    back = lax.dot_general(w2[...], delta_2, leading, preferred_element_type=F32)
    delta_1 = (back * slope_of(linear_1, sigmoid_1)).astype(jnp.bfloat16)
    grad_1 = lax.dot_general(delta_1, inputs, contract, preferred_element_type=F32)
    grad_2 = lax.dot_general(delta_2, hidden_1, contract, preferred_element_type=F32)
    grad_3 = lax.dot_general(hidden_2, error, contract, preferred_element_type=F32)
    outputs = grad_3.shape[1]
    row = lax.broadcasted_iota(jnp.int32, (outputs, 128), 0)
    lane = lax.broadcasted_iota(jnp.int32, (outputs, 128), 1)
    grad_3 = jnp.dot(
        grad_3, jnp.where(lane == row + THIRD_AT, 1.0, 0.0), precision=EXACT, preferred_element_type=F32
    )
    parts = (grad_1[:, :128], grad_1[:, 128:], grad_2[:, :128], grad_2[:, 128:])
    for i, part in enumerate(parts):
        rows = slice(256 * i, 256 * i + 256)
        layers[rows, :] = part if first else layers_in[rows, :] + part
    third[...] = grad_3 if first else third_in[...] + grad_3


def total_kernel(arrived, total):
    rows = arrived[0:8, :]
    for i in range(1, arrived.shape[0] // 8):
        rows = rows + arrived[8 * i : 8 * i + 8, :]
    total[...] = rows + pltpu.roll(rows, 4, 0)


def copy_kernel(total, copies):
    for i in range(copies.shape[0] // 8):
        copies[8 * i : 8 * i + 8, :] = total[...]


def normal_kernel(whole, first, second):
    for at, out in ((0, first), (512, second)):
        rows = whole[at : at + 512, :]
        square = jnp.sum(jnp.sum(rows * rows, axis=0, keepdims=True), axis=1, keepdims=True)
        scale = lax.rsqrt(square / (out.shape[0] * out.shape[1]) + epsilon)
        out[:, :128] = rows[:256] * scale
        out[:, 128:] = rows[256:] * scale


def body(
    right_side,
    diagonal,
    element_features,
    sample_bank,
    target_bank,
    patch_index,
    w_first,
    w_second,
    w_third,
):
    devices = lax.axis_size(GX_GZ_GA)
    table = tables()
    slots = (devices, 4, 128)
    count = patch_index.shape[0] // GROUPS
    weights_all = (w_first, w_second, w_third)

    def learn(number, held, waits):
        index = patch_index[count * number : count * number + count].reshape(1, count)
        return call(
            functools.partial(learn_kernel, number == 0), ((1024, 128), (devices, 128)), (),
            index, sample_bank, target_bank, *weights_all, *held,
            room=24, aliases={} if number == 0 else {6: 0, 7: 1}, waits=waits,
        )

    residual, precond, inverse, vector, *faces, token = call(
        start_kernel, (GRID,) * 4 + FACES, (), table, right_side, diagonal, element_features, *weights_all,
    )
    pressure = None
    weights, old_basis, old_images = None, [], []
    extra = jnp.zeros((8, 128), F32)
    gradient = ()
    for number, size in enumerate(BLOCKS):
        final = number + 1 == len(BLOCKS)
        old = len(old_basis)
        basis, images = [vector], []
        for j in range(size - 1):
            halo = exchange(faces)
            waits = ()
            if number == 0 and j < GROUPS:
                *gradient, done = learn(j, gradient, (token,))
                waits = (done,)
                if j == GROUPS - 1:
                    arrived = all_rows(gradient[0].reshape(slots)).reshape(1024, 128)
            if number == 1 and j == 0:
                whole = all_rows(copies.reshape(slots)).reshape(1024, 128)
            if number == 1 and j == 3:
                step_first, step_second, done = call(
                    normal_kernel, (w_first.shape, w_second.shape), (), whole, waits=(token,)
                )
                waits = (done,)
            image, vector, *faces, token = call(
                functools.partial(step_kernel, j == 0), (GRID, GRID) + FACES, HALO_SCRATCH,
                table, basis[-1], basis[max(j - 1, 0)], precond, inverse, *halo, waits=waits,
            )
            basis.append(vector)
            images.append(image)
        halo = exchange(faces)
        waits = ()
        if number == 0:
            total, done = call(total_kernel, (TOKEN,), (), arrived, waits=(token,))
            waits = (done,)
            extra = gradient[1]
        image, rows, token = call(
            functools.partial(last_kernel, size, old), (GRID, (devices, 128)), HALO_SCRATCH + ((128, 128),),
            table, precond, residual, extra, *halo, *basis, *images, *old_basis, waits=waits,
        )
        images.append(image)
        rows = all_rows(rows)
        given = [rows, table, residual, *basis, *images]
        shapes = [GRID, GRID]
        if old:
            given += [pressure, weights, *old_basis, *old_images]
        if final:
            shapes += [w_third.shape]
        else:
            given += [inverse]
            shapes += [GRID, *FACES, (64, 128), (8, 128)]
            if old:
                shapes += [GRID] * (2 * size)
        pressure, residual, *more, token = call(
            functools.partial(update_kernel, size, old, final), shapes, ((128, 128),), *given
        )
        if final:
            step_third = more[0]
        else:
            vector, faces, weights, extra = more[0], more[1:7], more[7], more[8]
            old_basis, old_images = basis, images
            if old:
                old_basis, old_images = more[9 : 9 + size], more[9 + size :]
        if number == 0:
            copies, _ = call(copy_kernel, ((1024, 128),), (), total, waits=(token,))
    return (pressure, residual, step_first, step_second, step_third)


def solution(mesh):
    finer = Mesh(
        mesh.devices.reshape(4, 2, 2, mesh.shape["gz"], mesh.shape["ga"]),
        GX_GZ_GA,
    )
    return jax.shard_map(
        body,
        mesh=finer,
        in_specs=(
            P(GX, "ga", "gz"),
            P(GX, "ga", "gz"),
            P(None, GX_GZ_GA),
            P(None, GX_GZ_GA),
            P(None, GX_GZ_GA),
            P(GX_GZ_GA),
            P(),
            P(),
            P(),
        ),
        out_specs=(P(GX, "ga", "gz"), P(GX, "ga", "gz"), P(), P(), P()),
        check_vma=False,
    )
```

```python
import functools

import jax
import jax.numpy as jnp
from jax import lax
from jax.experimental import pallas as pl
from jax.experimental.pallas import tpu as pltpu
from jax.sharding import Mesh
from jax.sharding import PartitionSpec as P

EL = 8
BLOCKS = (6, 6)
GROUPS = 4
GX = ("gx_0", "gx_1", "gx_2")
GX_GZ_GA = ("gx_0", "gx_1", "gx_2", "gz", "ga")
SAME_CORE = ("gx_0", "gx_1", "gz", "ga")

taps = (1.6, -0.2, 8.0 / 315.0, -1.0 / 560.0)
center = 3.0 * 205.0 / 72.0
epsilon = 1e-06
MIDDLE = 1.075
HALF = 0.925
THIRD_AT = 112
EXACT = lax.Precision.HIGHEST
F32 = jnp.float32
VMEM = pl.BlockSpec(memory_space=pltpu.VMEM)
TOKEN = (8, 128)


def after(kernel, count, waits, token, *refs):
    kernel(*refs[:count], *refs[count + waits : token], *refs[token + 1 :])
    refs[token][...] = jnp.zeros(TOKEN, F32)


def call(kernel, out_shapes, scratch, *args, room=14, aliases={}, waits=()):
    scratch = [pltpu.VMEM(s, F32) for s in scratch]
    out_shapes = (*out_shapes, TOKEN)
    count = len(args)
    args = (*args, *waits)
    kernel = functools.partial(after, kernel, count, len(waits), len(args) + len(out_shapes) - 1)
    return pl.pallas_call(
        kernel,
        out_shape=[jax.ShapeDtypeStruct(s, F32) for s in out_shapes],
        in_specs=[VMEM] * len(args),
        out_specs=[VMEM] * len(out_shapes),
        scratch_shapes=scratch,
        input_output_aliases=aliases,
        compiler_params=pltpu.CompilerParams(vmem_limit_bytes=room * 1024 * 1024),
    )(*args)


def pairs(count, odd):
    found = []
    for a in range(odd, count, 2):
        b = (a + 1) % count
        found += [(a, b), (b, a)]
    return found


def exchange(faces):
    xa, xb, ya, yb, za, zb = faces
    nx, ny, nz = lax.axis_size(GX), lax.axis_size("ga"), lax.axis_size("gz")
    return (
        lax.ppermute(xa, GX, pairs(nx, 0)),
        lax.ppermute(xb, GX, pairs(nx, 1)),
        lax.ppermute(ya, "ga", pairs(ny, 0)),
        lax.ppermute(yb, "ga", pairs(ny, 1)),
        lax.ppermute(za, "gz", pairs(nz, 0)),
        lax.ppermute(zb, "gz", pairs(nz, 1)),
    )


def tap_of(distance):
    distance = jnp.abs(distance)
    value = jnp.zeros(distance.shape, F32)
    for offset in range(1, 5):
        value = jnp.where(distance == offset, F32(taps[offset - 1]), value)
    return value


FLAGS, SELECT, SPREAD, BAND = 0, 8, 24, 40


def tables():
    rows = []
    even = {}
    inner = {}
    for name, axis in (("x", GX), ("y", "ga"), ("z", "gz")):
        index, count = lax.axis_index(axis), lax.axis_size(axis)
        even[name] = index % 2 == 0
        inner[name] = (index != 0) & (index != count - 1)
        rows += [even[name], inner[name]]
    rows += [even["x"], even["x"]]
    flags = jnp.broadcast_to(jnp.stack(rows).astype(F32)[:, None], (8, 128))
    row = lax.broadcasted_iota(jnp.int32, (16, 128), 0)
    lane = lax.broadcasted_iota(jnp.int32, (16, 128), 1)
    inside = row % 8
    upper = (row < 8) == even["z"]
    used = inside < 4
    select = jnp.where(used & (lane == inside + jnp.where(upper, 124, 0)), 1.0, 0.0)
    place = inside + jnp.where(upper, 128, -4)
    allowed = used & ((row < 8) | inner["z"])
    spread = jnp.where(allowed, tap_of(lane - place), 0.0)
    out = lax.broadcasted_iota(jnp.int32, (128, 128), 0)
    within = lax.broadcasted_iota(jnp.int32, (128, 128), 1)
    return jnp.concatenate([flags, select, spread, tap_of(out - within)], axis=0)


FACES = ((4, 32, 128), (4, 32, 128), (16, 4, 128), (16, 4, 128), (8, 512), (8, 512))
GRID = (16, 32, 128)


def write_faces(table, field, faces):
    xa, xb, ya, yb, za, zb = faces
    even_x = table[0:1, :] > 0.5
    even_y = table[2:3, :] > 0.5
    xa[...] = jnp.where(even_x, field[12:16], field[0:4])
    xb[...] = jnp.where(even_x, field[0:4], field[12:16])
    ya[...] = jnp.where(even_y, field[:, 28:32, :], field[:, 0:4, :])
    yb[...] = jnp.where(even_y, field[:, 0:4, :], field[:, 28:32, :])
    flat = field[...].reshape(512, 128)
    both = lax.dot_general(
        table[SELECT : SELECT + 16, :], flat, (((1,), (1,)), ((), ())),
        precision=EXACT, preferred_element_type=F32,
    )
    za[...] = both[0:8]
    zb[...] = both[8:16]


def image_planes(table, field, halo, xs, ys, zs, use):
    xa, xb, ya, yb, za, zb = halo
    even_x = table[0:1, :] > 0.5
    keep_x = table[1:2, :] > 0.5
    even_y = table[2:3, :] > 0.5
    keep_y = table[3:4, :] > 0.5
    outer = jnp.where(keep_x, xb[...], 0.0)
    xs[0:4] = jnp.where(even_x, outer, xa[...])
    xs[4:8] = jnp.where(even_x, xa[...], outer)
    outer = jnp.where(keep_y, yb[...], 0.0)
    ys[:, 4:8, :] = jnp.where(even_y, outer, ya[...])
    ys[:, 40:44, :] = jnp.where(even_y, ya[...], outer)
    ys[:, 8:40, :] = field[...]
    flat = field[...].reshape(512, 128)
    arrived = jnp.concatenate([za[...], zb[...]], axis=0)
    zs[...] = jnp.dot(
        flat, table[BAND : BAND + 128, :], precision=EXACT, preferred_element_type=F32
    ) + lax.dot_general(
        arrived, table[SPREAD : SPREAD + 16, :], (((0,), (0,)), ((), ())),
        precision=EXACT, preferred_element_type=F32,
    )

    def plane(i):
        if i < 0:
            return xs[i + 4]
        if i >= 16:
            return xs[i - 12]
        return field[i]

    for i in range(16):
        total = zs[32 * i : 32 * i + 32, :]
        for k in range(1, 5):
            along = (plane(i + k) + plane(i - k)) + (
                ys[i, 8 + k : 40 + k, :] + ys[i, 8 - k : 40 - k, :]
            )
            total = total + taps[k - 1] * along
        use(i, total)


HALO_SCRATCH = ((8, 32, 128), (16, 48, 128), (512, 128))


def start_kernel(table, right, diag, feats, w1, w2, w3, *rest):
    source, precond, inverse, basis = rest[:4]
    faces = rest[4:10]
    hidden = jnp.dot(w1[...], feats[...], preferred_element_type=F32)
    hidden = jax.nn.silu(hidden).astype(jnp.bfloat16)
    hidden = jnp.dot(w2[...], hidden, preferred_element_type=F32)
    hidden = jax.nn.silu(hidden).astype(jnp.bfloat16)
    stress = jnp.dot(w3[...], hidden, preferred_element_type=F32)
    trace = (stress[0:1] + stress[1:2] + stress[2:3]) / 3.0
    row = lax.broadcasted_iota(jnp.int32, (8, 128), 0)
    lane = lax.broadcasted_iota(jnp.int32, (8, 128), 1)
    apart = jnp.where(lane // 16 == row, trace, 0.0)
    element = lax.broadcasted_iota(jnp.int32, (128, 128), 0)
    node = lax.broadcasted_iota(jnp.int32, (128, 128), 1)
    widen = jnp.where(element % 16 == node // EL, 1.0, 0.0)
    wide = jnp.dot(apart, widen, precision=EXACT, preferred_element_type=F32)
    for i in range(16):
        for j in range(4):
            at = (i // EL) * 4 + j
            rows = slice(EL * j, EL * j + EL)
            value = right[i, rows, :] + wide[at : at + 1, :]
            weight = diag[i, rows, :] + center
            source[i, rows, :] = value
            precond[i, rows, :] = weight
            inverted = 1.0 / weight
            inverse[i, rows, :] = inverted
            basis[i, rows, :] = value * inverted
    write_faces(table, basis, faces)


def step_kernel(first, table, field, before, precond, inverse, *rest):
    halo, rest = rest[:6], rest[6:]
    image, after = rest[:2]
    faces, scratch = rest[2:8], rest[8:]

    def use(i, total):
        value = field[i]
        image[i] = precond[i] * value - total
        if first:
            after[i] = ((1.0 - MIDDLE) * value - total * inverse[i]) * (1.0 / HALF)
        else:
            after[i] = ((1.0 - MIDDLE) * value - total * inverse[i]) * (2.0 / HALF) - before[i]

    image_planes(table, field, halo, *scratch, use)
    write_faces(table, after, faces)


def products(size, old):
    wanted = [(("t", i), ("q", j)) for i in range(size) for j in range(i, size)]
    wanted += [(("t", i), ("r", 0)) for i in range(size)]
    groups = [wanted]
    if old:
        for i0 in range(0, old, 4):
            some = range(i0, min(old, i0 + 4))
            groups.append([(("p", i), ("q", j)) for i in some for j in range(size)] + [(("p", i), ("r", 0)) for i in some])
    return groups


def last_kernel(size, old, table, precond, residual, *rest):
    halo, rest = rest[:6], rest[6:]
    basis, rest = rest[:size], rest[size:]
    images, rest = rest[: size - 1], rest[size - 1 :]
    olds, rest = rest[:old], rest[old:]
    image, row = rest[:2]
    scratch, sums = rest[2:5], rest[5]
    field = basis[-1]

    def use(i, total):
        image[i] = precond[i] * field[i] - total

    image_planes(table, field, halo, *scratch, use)
    refs = {("r", 0): residual}
    for j in range(size):
        refs["t", j] = basis[j]
        refs["q", j] = images[j] if j < size - 1 else image
    for j in range(old):
        refs["p", j] = olds[j]
    sums[...] = jnp.zeros(sums.shape, F32)
    at = 0
    for group in products(size, old):
        names = sorted({name for pair in group for name in pair})

        def add(i, totals, names=names, group=group):
            for part in range(4):
                value = {n: refs[n][i, 8 * part : 8 * part + 8, :] for n in names}
                totals = tuple(
                    total + value[a] * value[b] for total, (a, b) in zip(totals, group)
                )
            return totals

        totals = lax.fori_loop(0, 16, add, (jnp.zeros((8, 128), F32),) * len(group))
        for total in totals:
            sums[at : at + 1, :] = jnp.sum(total, axis=0, keepdims=True)
            at += 1
    row[...] = lax.dot_general(
        jnp.ones((8, 128), F32), sums[...], (((1,), (1,)), ((), ())),
        precision=EXACT, preferred_element_type=F32,
    )


def factor(matrix, size):
    low, scaled, inverse = {}, {}, []
    for j in range(size):
        pivot = matrix[j][j]
        for k in range(j):
            pivot = pivot - low[j, k] * scaled[j, k]
        inverse.append(1.0 / pivot)
        for i in range(j + 1, size):
            value = matrix[i][j]
            for k in range(j):
                value = value - scaled[i, k] * low[j, k]
            scaled[i, j] = value
            low[i, j] = value * inverse[j]
    return low, inverse


def solve(factors, size, right):
    low, inverse = factors
    found = []
    for i in range(size):
        value = right[i]
        for k in range(i):
            value = value - low[i, k] * found[k]
        found.append(value)
    found = [a * b for a, b in zip(found, inverse)]
    for i in reversed(range(size)):
        for k in range(i + 1, size):
            found[i] = found[i] - low[k, i] * found[k]
    return found


def update_kernel(size, old, final, *rest):
    gathered, table, residual, rest = rest[0], rest[1], rest[2], rest[3:]
    basis, rest = rest[:size], rest[size:]
    images, rest = rest[:size], rest[size:]
    if old:
        pressure, weights, rest = rest[0], rest[1], rest[2:]
        old_basis, rest = rest[:old], rest[old:]
        old_images, rest = rest[:old], rest[old:]
    if not final:
        inverse, rest = rest[0], rest[1:]
    new_pressure, new_residual = rest[:2]
    rest = rest[2:]
    if not final:
        after, faces, new_weights, share, rest = rest[0], rest[1:7], rest[7], rest[8], rest[9:]
        if old:
            new_basis, rest = rest[:size], rest[size:]
            new_images, rest = rest[:size], rest[size:]
    splats = rest[0]
    total = gathered[0:8, :]
    for i in range(1, gathered.shape[0] // 8):
        total = total + gathered[8 * i : 8 * i + 8, :]
    totals = total[4:5, :]
    row = lax.broadcasted_iota(jnp.int32, (128, 128), 0)
    lane = lax.broadcasted_iota(jnp.int32, (128, 128), 1)
    splats[...] = jnp.dot(
        jnp.where((row == lane) & (lane < THIRD_AT), totals, 0.0), jnp.ones((128, 128), F32),
        precision=EXACT, preferred_element_type=F32,
    )
    if not final:
        share[...] = total
    value = {}
    at = 0
    for group in products(size, old):
        for a, b in group:
            value[a, b] = splats[at : at + 1, :]
            at += 1
    gram = [[value[("t", min(i, j)), ("q", max(i, j))] for j in range(size)] for i in range(size)]
    right = [value[("t", i), ("r", 0)] for i in range(size)]
    mix = None
    if old:
        cross = [[value[("p", i), ("q", j)] for j in range(size)] for i in range(old)]
        held = [[weights[i * old + j : i * old + j + 1, :] for j in range(old)] for i in range(old)]
        factors = factor(held, old)
        columns = [solve(factors, old, [-cross[i][j] for i in range(old)]) for j in range(size)]
        behind = [value[("p", i), ("r", 0)] for i in range(old)]
        for j in range(size):
            for k in range(old):
                right[j] = right[j] + columns[j][k] * behind[k]
        behind = solve(factors, old, behind)
        for i in range(size):
            for j in range(i, size):
                for k in range(old):
                    gram[i][j] = gram[i][j] + cross[k][i] * columns[j][k]
                gram[j][i] = gram[i][j]
        mix = [[jnp.broadcast_to(v, (8, 128)) for v in column] for column in columns]
    step = solve(factor(gram, size), size, right)
    if not final:
        new_weights[...] = jnp.zeros(new_weights.shape, F32)
        for i in range(size):
            for j in range(size):
                new_weights[i * size + j : i * size + j + 1, :] = gram[i][j]
    if old:
        carried = []
        for i in range(old):
            total = behind[i]
            if final:
                for j in range(size):
                    total = total + step[j] * columns[j][i]
            carried.append(jnp.broadcast_to(total, (8, 128)))
    step = [jnp.broadcast_to(v, (8, 128)) for v in step]

    def tile(i, part):
        rows = slice(8 * part, 8 * part + 8)
        vectors = [ref[i, rows, :] for ref in basis]
        duals = [ref[i, rows, :] for ref in images]
        if old and not final:
            held_v = [ref[i, rows, :] for ref in old_basis]
            held_d = [ref[i, rows, :] for ref in old_images]
            for j in range(size):
                for k in range(old):
                    vectors[j] = vectors[j] + mix[j][k] * held_v[k]
                    duals[j] = duals[j] + mix[j][k] * held_d[k]
                new_basis[j][i, rows, :] = vectors[j]
                new_images[j][i, rows, :] = duals[j]
        gain = step[0] * vectors[0]
        loss = step[0] * duals[0]
        for j in range(1, size):
            gain = gain + step[j] * vectors[j]
            loss = loss + step[j] * duals[j]
        if old:
            for k in range(old):
                gain = gain + carried[k] * old_basis[k][i, rows, :]
                loss = loss + carried[k] * old_images[k][i, rows, :]
        if old:
            gain = pressure[i, rows, :] + gain
        left = residual[i, rows, :] - loss
        new_pressure[i, rows, :] = gain
        new_residual[i, rows, :] = left
        if not final:
            after[i, rows, :] = left * inverse[i, rows, :]

    def planes(i, nothing):
        for part in range(4):
            tile(i, part)
        return nothing

    lax.fori_loop(0, 16, planes, 0)
    if not final:
        write_faces(table, after, faces)


def all_slots(slots):
    return lax.all_to_all(slots, SAME_CORE, split_axis=0, concat_axis=0, tiled=True)


def other_core(array):
    return lax.ppermute(array, GX[-1], pairs(2, 0))


def slope_of(linear, sigmoid):
    return sigmoid * (1.0 + linear * (1.0 - sigmoid))


def learn_kernel(first, index, bank, target, w1, w2, w3, *rest):
    if not first:
        layers_in, third_in, rest = rest[0], rest[1], rest[2:]
    layers, third = rest
    group = index.shape[1]
    column = lax.broadcasted_iota(jnp.int32, (bank.shape[1], group), 0)
    chosen = jnp.where(column == index[...], 1.0, 0.0).astype(jnp.bfloat16)
    inputs = jnp.dot(bank[...], chosen, preferred_element_type=F32).astype(jnp.bfloat16)
    wanted = jnp.dot(target[...], chosen, preferred_element_type=F32)
    linear_1 = jnp.dot(w1[...], inputs, preferred_element_type=F32)
    sigmoid_1 = 1.0 / (1.0 + jnp.exp(-linear_1))
    hidden_1 = (linear_1 * sigmoid_1).astype(jnp.bfloat16)
    linear_2 = jnp.dot(w2[...], hidden_1, preferred_element_type=F32)
    sigmoid_2 = 1.0 / (1.0 + jnp.exp(-linear_2))
    hidden_2 = (linear_2 * sigmoid_2).astype(jnp.bfloat16)
    stress = jnp.dot(w3[...], hidden_2, preferred_element_type=F32)
    error = (stress - wanted).astype(jnp.bfloat16)
    contract = (((1,), (1,)), ((), ()))
    leading = (((0,), (0,)), ((), ()))
    back = lax.dot_general(w3[...], error, leading, preferred_element_type=F32)
    delta_2 = (back * slope_of(linear_2, sigmoid_2)).astype(jnp.bfloat16)
    back = lax.dot_general(w2[...], delta_2, leading, preferred_element_type=F32)
    delta_1 = (back * slope_of(linear_1, sigmoid_1)).astype(jnp.bfloat16)
    grad_1 = lax.dot_general(delta_1, inputs, contract, preferred_element_type=F32)
    grad_2 = lax.dot_general(delta_2, hidden_1, contract, preferred_element_type=F32)
    grad_3 = lax.dot_general(hidden_2, error, contract, preferred_element_type=F32)
    outputs = grad_3.shape[1]
    row = lax.broadcasted_iota(jnp.int32, (outputs, 128), 0)
    lane = lax.broadcasted_iota(jnp.int32, (outputs, 128), 1)
    grad_3 = jnp.dot(
        grad_3, jnp.where(lane == row + THIRD_AT, 1.0, 0.0), precision=EXACT, preferred_element_type=F32
    )
    parts = (grad_1[:, :128], grad_1[:, 128:], grad_2[:, :128], grad_2[:, 128:])
    for i, part in enumerate(parts):
        rows = slice(256 * i, 256 * i + 256)
        layers[rows, :] = part if first else layers_in[rows, :] + part
    third[...] = grad_3 if first else third_in[...] + grad_3


def split_kernel(table, layers, third, mine, other):
    first = table[0:1, :] > 0.5
    for ref, at, rows in ((layers, 0, 512), (third, 512, 128)):
        low, high = ref[0:rows, :], ref[rows : 2 * rows, :]
        mine[at : at + rows, :] = jnp.where(first, low, high)
        other[at : at + rows, :] = jnp.where(first, high, low)


def pack_kernel(row, row_other, mine, other, slots):
    upper = lax.broadcasted_iota(jnp.int32, (8, 128), 0) < 4
    inner = row[...] + row_other[...]
    for i in range(slots.shape[0] // 16):
        rows = slice(8 * i, 8 * i + 8)
        tile = mine[rows, :] + other[rows, :]
        for j in range(2):
            at = slice(512 + 2 * i + j, 512 + 2 * i + j + 1)
            below = inner + (mine[at, :] + other[at, :])
            slots[16 * i + 8 * j : 16 * i + 8 * j + 8, :] = jnp.where(upper, pltpu.roll(tile, 4, 0) if j else tile, below)


def pack_again_kernel(row, row_other, share, slots):
    upper = lax.broadcasted_iota(jnp.int32, (8, 128), 0) < 4
    lane = lax.broadcasted_iota(jnp.int32, (8, 128), 1)
    tile = jnp.where(upper | (lane >= THIRD_AT), share[...], row[...] + row_other[...])
    for i in range(slots.shape[0] // 8):
        slots[8 * i : 8 * i + 8, :] = tile


def normal_kernel(table, mine, other, first, second, third, rows, columns):
    low = table[0:1, :] > 0.5
    upper = lax.broadcasted_iota(jnp.int32, (8, 128), 0) < 4
    for i in range(64):
        tiles = []
        for ref in (mine, other):
            tiles.append(
                jnp.where(upper, ref[16 * i : 16 * i + 8, :], pltpu.roll(ref[16 * i + 8 : 16 * i + 16, :], 4, 0))
            )
        rows[8 * i : 8 * i + 8, :] = jnp.where(low, tiles[0], tiles[1])
        rows[512 + 8 * i : 512 + 8 * i + 8, :] = jnp.where(low, tiles[1], tiles[0])
    for at, out in ((0, first), (512, second)):
        part = rows[at : at + 512, :]
        square = jnp.sum(jnp.sum(part * part, axis=0, keepdims=True), axis=1, keepdims=True)
        scale = lax.rsqrt(square / (out.shape[0] * out.shape[1]) + epsilon)
        out[:, :128] = part[:256] * scale
        out[:, 128:] = part[256:] * scale
    own, its = mine[pl.ds(4, 128, stride=8), :], other[pl.ds(4, 128, stride=8), :]
    columns[0:128, :] = jnp.where(low, own, its)
    columns[128:256, :] = jnp.where(low, its, own)
    outputs, channels = third.shape
    row = lax.broadcasted_iota(jnp.int32, (8, 128), 0)
    lane = lax.broadcasted_iota(jnp.int32, (8, 128), 1)
    taken = lax.dot_general(
        jnp.where((lane == row + THIRD_AT) & (row < outputs), 1.0, 0.0), columns[...],
        (((1,), (1,)), ((), ())), precision=EXACT, preferred_element_type=F32,
    )
    square = jnp.sum(jnp.sum(taken * taken, axis=0, keepdims=True), axis=1, keepdims=True)
    taken = taken * lax.rsqrt(square / (outputs * channels) + epsilon)
    third[...] = taken[:outputs]


def body(
    right_side,
    diagonal,
    element_features,
    sample_bank,
    target_bank,
    patch_index,
    w_first,
    w_second,
    w_third,
):
    devices = lax.axis_size(GX_GZ_GA)
    table = tables()
    count = patch_index.shape[0] // GROUPS
    layer_weights = (w_first, w_second, w_third)

    def learn(number, held, waits):
        index = patch_index[count * number : count * number + count].reshape(1, count)
        return call(
            functools.partial(learn_kernel, number == 0), ((1024, 128), (256, 128)), (),
            index, sample_bank, target_bank, *layer_weights, *held,
            room=24, aliases={} if number == 0 else {6: 0, 7: 1}, waits=waits,
        )

    residual, precond, inverse, vector, *faces, token = call(
        start_kernel, (GRID,) * 4 + FACES, (), table, right_side, diagonal, element_features, *layer_weights,
    )
    pressure = share = None
    weights, old_basis, old_images = None, [], []
    gradient = ()
    slots = (8 * devices // 2, 128)
    for number, size in enumerate(BLOCKS):
        final = number + 1 == len(BLOCKS)
        old = len(old_basis)
        basis, images = [vector], []
        for j in range(size - 1):
            halo = exchange(faces)
            waits = ()
            if number == 0 and j < GROUPS:
                *gradient, done = learn(j, gradient, (token,))
                waits = (done,)
            image, vector, *faces, token = call(
                functools.partial(step_kernel, j == 0), (GRID, GRID) + FACES, HALO_SCRATCH,
                table, basis[-1], basis[max(j - 1, 0)], precond, inverse, *halo, waits=waits,
            )
            if number == 0 and j == GROUPS - 1:
                mine, other, _ = call(split_kernel, ((640, 128),) * 2, (), table, *gradient)
                other = other_core(other)
            basis.append(vector)
            images.append(image)
        halo = exchange(faces)
        image, row, _ = call(
            functools.partial(last_kernel, size, old), (GRID, (8, 128)), HALO_SCRATCH + ((128, 128),),
            table, precond, residual, *halo, *basis, *images, *old_basis,
        )
        images.append(image)
        if number == 0:
            packed, _ = call(pack_kernel, (slots,), (), row, other_core(row), mine, other)
        else:
            packed, _ = call(pack_again_kernel, (slots,), (), row, other_core(row), share)
        gathered = all_slots(packed)
        given = [gathered, table, residual, *basis, *images]
        shapes = [GRID, GRID]
        if old:
            given += [pressure, weights, *old_basis, *old_images]
        if not final:
            given += [inverse]
            shapes += [GRID, *FACES, (64, 128), (8, 128)]
            if old:
                shapes += [GRID] * (2 * size)
        pressure, residual, *more, token = call(
            functools.partial(update_kernel, size, old, final), shapes, ((128, 128),), *given
        )
        if not final:
            vector, faces, weights, share = more[0], more[1:7], more[7], more[8]
            old_basis, old_images = basis, images
            if old:
                old_basis, old_images = more[9 : 9 + size], more[9 + size :]
    step_first, step_second, step_third, _ = call(
        normal_kernel, (w_first.shape, w_second.shape, w_third.shape), ((1024, 128), (256, 128)),
        table, gathered, other_core(gathered),
    )
    return (pressure, residual, step_first, step_second, step_third)


def solution(mesh):
    finer = Mesh(
        mesh.devices.reshape(4, 2, 2, mesh.shape["gz"], mesh.shape["ga"]),
        GX_GZ_GA,
    )
    return jax.shard_map(
        body,
        mesh=finer,
        in_specs=(
            P(GX, "ga", "gz"),
            P(GX, "ga", "gz"),
            P(None, GX_GZ_GA),
            P(None, GX_GZ_GA),
            P(None, GX_GZ_GA),
            P(GX_GZ_GA),
            P(),
            P(),
            P(),
        ),
        out_specs=(P(GX, "ga", "gz"), P(GX, "ga", "gz"), P(), P(), P()),
        check_vma=False,
    )
```

```python
import functools

import jax
import jax.numpy as jnp
from jax import lax
from jax.experimental import pallas as pl
from jax.experimental.pallas import tpu as pltpu
from jax.sharding import Mesh
from jax.sharding import PartitionSpec as P

EL = 8
BLOCKS = (6, 6)
GROUPS = 4
GX = ("gx_0", "gx_1", "gx_2")
GX_GZ_GA = ("gx_0", "gx_1", "gx_2", "gz", "ga")
SAME_CORE = ("gx_0", "gx_1", "gz", "ga")

taps = (1.6, -0.2, 8.0 / 315.0, -1.0 / 560.0)
center = 3.0 * 205.0 / 72.0
epsilon = 1e-06
MIDDLE = 1.075
HALF = 0.925
THIRD_AT = 112
EXACT = lax.Precision.HIGHEST
F32 = jnp.float32
VMEM = pl.BlockSpec(memory_space=pltpu.VMEM)
TOKEN = (8, 128)


def after(kernel, count, waits, token, *refs):
    given = refs[:count] + refs[count + waits :]
    if token:
        refs[token][...] = jnp.zeros(TOKEN, F32)
        given = refs[:count] + refs[count + waits : token] + refs[token + 1 :]
    kernel(*given)


def call(kernel, out_shapes, scratch, *args, room=14, aliases={}, waits=(), token=False):
    scratch = [pltpu.VMEM(s, F32) for s in scratch]
    count = len(args)
    args = (*args, *waits)
    out_shapes = (*out_shapes, TOKEN) if token else out_shapes
    kernel = functools.partial(after, kernel, count, len(waits), token and len(args) + len(out_shapes) - 1)
    return pl.pallas_call(
        kernel,
        out_shape=[jax.ShapeDtypeStruct(s, F32) for s in out_shapes],
        in_specs=[VMEM] * len(args),
        out_specs=[VMEM] * len(out_shapes),
        scratch_shapes=scratch,
        input_output_aliases=aliases,
        compiler_params=pltpu.CompilerParams(vmem_limit_bytes=room * 1024 * 1024),
    )(*args)


def pairs(count, odd):
    found = []
    for a in range(odd, count, 2):
        b = (a + 1) % count
        found += [(a, b), (b, a)]
    return found


def exchange(faces):
    xa, xb, ya, yb, za, zb = faces
    nx, ny, nz = lax.axis_size(GX), lax.axis_size("ga"), lax.axis_size("gz")
    return (
        lax.ppermute(xa, GX, pairs(nx, 0)),
        lax.ppermute(xb, GX, pairs(nx, 1)),
        lax.ppermute(ya, "ga", pairs(ny, 0)),
        lax.ppermute(yb, "ga", pairs(ny, 1)),
        lax.ppermute(za, "gz", pairs(nz, 0)),
        lax.ppermute(zb, "gz", pairs(nz, 1)),
    )


def tap_of(distance):
    distance = jnp.abs(distance)
    value = jnp.zeros(distance.shape, F32)
    for offset in range(1, 5):
        value = jnp.where(distance == offset, F32(taps[offset - 1]), value)
    return value


FLAGS, SELECT, SPREAD, BAND = 0, 8, 24, 40


def tables():
    rows = []
    even = {}
    inner = {}
    for name, axis in (("x", GX), ("y", "ga"), ("z", "gz")):
        index, count = lax.axis_index(axis), lax.axis_size(axis)
        even[name] = index % 2 == 0
        inner[name] = (index != 0) & (index != count - 1)
        rows += [even[name], inner[name]]
    rows += [even["x"], even["x"]]
    flags = jnp.broadcast_to(jnp.stack(rows).astype(F32)[:, None], (8, 128))
    row = lax.broadcasted_iota(jnp.int32, (16, 128), 0)
    lane = lax.broadcasted_iota(jnp.int32, (16, 128), 1)
    inside = row % 8
    upper = (row < 8) == even["z"]
    used = inside < 4
    select = jnp.where(used & (lane == inside + jnp.where(upper, 124, 0)), 1.0, 0.0)
    place = inside + jnp.where(upper, 128, -4)
    allowed = used & ((row < 8) | inner["z"])
    spread = jnp.where(allowed, tap_of(lane - place), 0.0)
    out = lax.broadcasted_iota(jnp.int32, (128, 128), 0)
    within = lax.broadcasted_iota(jnp.int32, (128, 128), 1)
    return jnp.concatenate([flags, select, spread, tap_of(out - within)], axis=0)


FACES = ((4, 32, 128), (4, 32, 128), (16, 4, 128), (16, 4, 128), (8, 512), (8, 512))
GRID = (16, 32, 128)


def write_faces(table, field, faces):
    xa, xb, ya, yb, za, zb = faces
    even_x = table[0:1, :] > 0.5
    even_y = table[2:3, :] > 0.5
    xa[...] = jnp.where(even_x, field[12:16], field[0:4])
    xb[...] = jnp.where(even_x, field[0:4], field[12:16])
    ya[...] = jnp.where(even_y, field[:, 28:32, :], field[:, 0:4, :])
    yb[...] = jnp.where(even_y, field[:, 0:4, :], field[:, 28:32, :])
    flat = field[...].reshape(512, 128)
    both = lax.dot_general(
        table[SELECT : SELECT + 16, :], flat, (((1,), (1,)), ((), ())),
        precision=EXACT, preferred_element_type=F32,
    )
    za[...] = both[0:8]
    zb[...] = both[8:16]


def image_planes(table, field, halo, xs, ys, zs, use):
    xa, xb, ya, yb, za, zb = halo
    even_x = table[0:1, :] > 0.5
    keep_x = table[1:2, :] > 0.5
    even_y = table[2:3, :] > 0.5
    keep_y = table[3:4, :] > 0.5
    outer = jnp.where(keep_x, xb[...], 0.0)
    xs[0:4] = jnp.where(even_x, outer, xa[...])
    xs[4:8] = jnp.where(even_x, xa[...], outer)
    outer = jnp.where(keep_y, yb[...], 0.0)
    ys[:, 4:8, :] = jnp.where(even_y, outer, ya[...])
    ys[:, 40:44, :] = jnp.where(even_y, ya[...], outer)
    ys[:, 8:40, :] = field[...]
    flat = field[...].reshape(512, 128)
    arrived = jnp.concatenate([za[...], zb[...]], axis=0)
    zs[...] = jnp.dot(
        flat, table[BAND : BAND + 128, :], precision=EXACT, preferred_element_type=F32
    ) + lax.dot_general(
        arrived, table[SPREAD : SPREAD + 16, :], (((0,), (0,)), ((), ())),
        precision=EXACT, preferred_element_type=F32,
    )

    def plane(i):
        if i < 0:
            return xs[i + 4]
        if i >= 16:
            return xs[i - 12]
        return field[i]

    for i in range(16):
        total = zs[32 * i : 32 * i + 32, :]
        for k in range(1, 5):
            along = (plane(i + k) + plane(i - k)) + (
                ys[i, 8 + k : 40 + k, :] + ys[i, 8 - k : 40 - k, :]
            )
            total = total + taps[k - 1] * along
        use(i, total)


HALO_SCRATCH = ((8, 32, 128), (16, 48, 128), (512, 128))


def start_kernel(table, right, diag, feats, w1, w2, w3, *rest):
    source, precond, inverse, basis = rest[:4]
    faces = rest[4:10]
    hidden = jnp.dot(w1[...], feats[...], preferred_element_type=F32)
    hidden = jax.nn.silu(hidden).astype(jnp.bfloat16)
    hidden = jnp.dot(w2[...], hidden, preferred_element_type=F32)
    hidden = jax.nn.silu(hidden).astype(jnp.bfloat16)
    stress = jnp.dot(w3[...], hidden, preferred_element_type=F32)
    trace = (stress[0:1] + stress[1:2] + stress[2:3]) / 3.0
    row = lax.broadcasted_iota(jnp.int32, (8, 128), 0)
    lane = lax.broadcasted_iota(jnp.int32, (8, 128), 1)
    apart = jnp.where(lane // 16 == row, trace, 0.0)
    element = lax.broadcasted_iota(jnp.int32, (128, 128), 0)
    node = lax.broadcasted_iota(jnp.int32, (128, 128), 1)
    widen = jnp.where(element % 16 == node // EL, 1.0, 0.0)
    wide = jnp.dot(apart, widen, precision=EXACT, preferred_element_type=F32)
    for i in range(16):
        for j in range(4):
            at = (i // EL) * 4 + j
            rows = slice(EL * j, EL * j + EL)
            value = right[i, rows, :] + wide[at : at + 1, :]
            weight = diag[i, rows, :] + center
            source[i, rows, :] = value
            precond[i, rows, :] = weight
            inverted = 1.0 / weight
            inverse[i, rows, :] = inverted
            basis[i, rows, :] = value * inverted
    write_faces(table, basis, faces)


def step_kernel(first, table, field, before, precond, inverse, *rest):
    halo, rest = rest[:6], rest[6:]
    image, after = rest[:2]
    faces, scratch = rest[2:8], rest[8:]

    def use(i, total):
        value = field[i]
        image[i] = precond[i] * value - total
        if first:
            after[i] = ((1.0 - MIDDLE) * value - total * inverse[i]) * (1.0 / HALF)
        else:
            after[i] = ((1.0 - MIDDLE) * value - total * inverse[i]) * (2.0 / HALF) - before[i]

    image_planes(table, field, halo, *scratch, use)
    write_faces(table, after, faces)


def products(size, old):
    wanted = [(("t", i), ("q", j)) for i in range(size) for j in range(i, size)]
    wanted += [(("t", i), ("r", 0)) for i in range(size)]
    groups = [wanted]
    if old:
        for i0 in range(0, old, 4):
            some = range(i0, min(old, i0 + 4))
            groups.append([(("p", i), ("q", j)) for i in some for j in range(size)] + [(("p", i), ("r", 0)) for i in some])
    return groups


def last_kernel(size, old, table, precond, residual, *rest):
    halo, rest = rest[:6], rest[6:]
    basis, rest = rest[:size], rest[size:]
    images, rest = rest[: size - 1], rest[size - 1 :]
    olds, rest = rest[:old], rest[old:]
    image, row = rest[:2]
    scratch, sums = rest[2:5], rest[5]
    field = basis[-1]

    def use(i, total):
        image[i] = precond[i] * field[i] - total

    image_planes(table, field, halo, *scratch, use)
    refs = {("r", 0): residual}
    for j in range(size):
        refs["t", j] = basis[j]
        refs["q", j] = images[j] if j < size - 1 else image
    for j in range(old):
        refs["p", j] = olds[j]
    sums[...] = jnp.zeros(sums.shape, F32)
    at = 0
    for group in products(size, old):
        names = sorted({name for pair in group for name in pair})

        def add(i, totals, names=names, group=group):
            for part in range(4):
                value = {n: refs[n][i, 8 * part : 8 * part + 8, :] for n in names}
                totals = tuple(
                    total + value[a] * value[b] for total, (a, b) in zip(totals, group)
                )
            return totals

        totals = lax.fori_loop(0, 16, add, (jnp.zeros((8, 128), F32),) * len(group))
        for total in totals:
            sums[at : at + 1, :] = jnp.sum(total, axis=0, keepdims=True)
            at += 1
    row[...] = lax.dot_general(
        jnp.ones((8, 128), F32), sums[...], (((1,), (1,)), ((), ())),
        precision=EXACT, preferred_element_type=F32,
    )


def factor(matrix, size):
    low, scaled, inverse = {}, {}, []
    for j in range(size):
        pivot = matrix[j][j]
        for k in range(j):
            pivot = pivot - low[j, k] * scaled[j, k]
        inverse.append(1.0 / pivot)
        for i in range(j + 1, size):
            value = matrix[i][j]
            for k in range(j):
                value = value - scaled[i, k] * low[j, k]
            scaled[i, j] = value
            low[i, j] = value * inverse[j]
    return low, inverse


def solve(factors, size, right):
    low, inverse = factors
    found = []
    for i in range(size):
        value = right[i]
        for k in range(i):
            value = value - low[i, k] * found[k]
        found.append(value)
    found = [a * b for a, b in zip(found, inverse)]
    for i in reversed(range(size)):
        for k in range(i + 1, size):
            found[i] = found[i] - low[k, i] * found[k]
    return found


def update_kernel(size, old, final, *rest):
    gathered, table, residual, rest = rest[0], rest[1], rest[2], rest[3:]
    basis, rest = rest[:size], rest[size:]
    images, rest = rest[:size], rest[size:]
    if old:
        pressure, weights, rest = rest[0], rest[1], rest[2:]
        old_basis, rest = rest[:old], rest[old:]
        old_images, rest = rest[:old], rest[old:]
    if not final:
        inverse, rest = rest[0], rest[1:]
    new_pressure, new_residual = rest[:2]
    rest = rest[2:]
    if not final:
        after, faces, new_weights, share, rest = rest[0], rest[1:7], rest[7], rest[8], rest[9:]
        if old:
            new_basis, rest = rest[:size], rest[size:]
            new_images, rest = rest[:size], rest[size:]
    splats = rest[0]
    total = gathered[0:8, :]
    for i in range(1, gathered.shape[0] // 8):
        total = total + gathered[8 * i : 8 * i + 8, :]
    totals = total[4:5, :]
    row = lax.broadcasted_iota(jnp.int32, (128, 128), 0)
    lane = lax.broadcasted_iota(jnp.int32, (128, 128), 1)
    splats[...] = jnp.dot(
        jnp.where((row == lane) & (lane < THIRD_AT), totals, 0.0), jnp.ones((128, 128), F32),
        precision=EXACT, preferred_element_type=F32,
    )
    if not final:
        share[...] = total
    value = {}
    at = 0
    for group in products(size, old):
        for a, b in group:
            value[a, b] = splats[at : at + 1, :]
            at += 1
    gram = [[value[("t", min(i, j)), ("q", max(i, j))] for j in range(size)] for i in range(size)]
    right = [value[("t", i), ("r", 0)] for i in range(size)]
    mix = None
    if old:
        cross = [[value[("p", i), ("q", j)] for j in range(size)] for i in range(old)]
        held = [[weights[i * old + j : i * old + j + 1, :] for j in range(old)] for i in range(old)]
        factors = factor(held, old)
        columns = [solve(factors, old, [-cross[i][j] for i in range(old)]) for j in range(size)]
        behind = [value[("p", i), ("r", 0)] for i in range(old)]
        for j in range(size):
            for k in range(old):
                right[j] = right[j] + columns[j][k] * behind[k]
        behind = solve(factors, old, behind)
        for i in range(size):
            for j in range(i, size):
                for k in range(old):
                    gram[i][j] = gram[i][j] + cross[k][i] * columns[j][k]
                gram[j][i] = gram[i][j]
        mix = [[jnp.broadcast_to(v, (8, 128)) for v in column] for column in columns]
    step = solve(factor(gram, size), size, right)
    if not final:
        new_weights[...] = jnp.zeros(new_weights.shape, F32)
        for i in range(size):
            for j in range(size):
                new_weights[i * size + j : i * size + j + 1, :] = gram[i][j]
    if old:
        carried = []
        for i in range(old):
            total = behind[i]
            if final:
                for j in range(size):
                    total = total + step[j] * columns[j][i]
            carried.append(jnp.broadcast_to(total, (8, 128)))
    step = [jnp.broadcast_to(v, (8, 128)) for v in step]

    def tile(i, part):
        rows = slice(8 * part, 8 * part + 8)
        vectors = [ref[i, rows, :] for ref in basis]
        duals = [ref[i, rows, :] for ref in images]
        if old and not final:
            held_v = [ref[i, rows, :] for ref in old_basis]
            held_d = [ref[i, rows, :] for ref in old_images]
            for j in range(size):
                for k in range(old):
                    vectors[j] = vectors[j] + mix[j][k] * held_v[k]
                    duals[j] = duals[j] + mix[j][k] * held_d[k]
                new_basis[j][i, rows, :] = vectors[j]
                new_images[j][i, rows, :] = duals[j]
        gain = step[0] * vectors[0]
        loss = step[0] * duals[0]
        for j in range(1, size):
            gain = gain + step[j] * vectors[j]
            loss = loss + step[j] * duals[j]
        if old:
            for k in range(old):
                gain = gain + carried[k] * old_basis[k][i, rows, :]
                loss = loss + carried[k] * old_images[k][i, rows, :]
        if old:
            gain = pressure[i, rows, :] + gain
        left = residual[i, rows, :] - loss
        new_pressure[i, rows, :] = gain
        new_residual[i, rows, :] = left
        if not final:
            after[i, rows, :] = left * inverse[i, rows, :]

    def planes(i, nothing):
        for part in range(4):
            tile(i, part)
        return nothing

    lax.fori_loop(0, 16, planes, 0)
    if not final:
        write_faces(table, after, faces)


def all_slots(slots):
    return lax.all_to_all(slots, SAME_CORE, split_axis=0, concat_axis=0, tiled=True)


def other_core(array):
    return lax.ppermute(array, GX[-1], pairs(2, 0))


def slope_of(linear, sigmoid):
    return sigmoid * (1.0 + linear * (1.0 - sigmoid))


def learn_kernel(number, group, index, bank, target, w1, w2, w3, *rest):
    first = number == 0
    if not first:
        layers_in, third_in, rest = rest[0], rest[1], rest[2:]
    layers, third = rest
    column = lax.broadcasted_iota(jnp.int32, (bank.shape[1], group), 0)
    chosen = jnp.where(column == index[:, group * number : group * number + group], 1.0, 0.0).astype(jnp.bfloat16)
    inputs = jnp.dot(bank[...], chosen, preferred_element_type=F32).astype(jnp.bfloat16)
    wanted = jnp.dot(target[...], chosen, preferred_element_type=F32)
    linear_1 = jnp.dot(w1[...], inputs, preferred_element_type=F32)
    sigmoid_1 = 1.0 / (1.0 + jnp.exp(-linear_1))
    hidden_1 = (linear_1 * sigmoid_1).astype(jnp.bfloat16)
    linear_2 = jnp.dot(w2[...], hidden_1, preferred_element_type=F32)
    sigmoid_2 = 1.0 / (1.0 + jnp.exp(-linear_2))
    hidden_2 = (linear_2 * sigmoid_2).astype(jnp.bfloat16)
    stress = jnp.dot(w3[...], hidden_2, preferred_element_type=F32)
    error = (stress - wanted).astype(jnp.bfloat16)
    contract = (((1,), (1,)), ((), ()))
    leading = (((0,), (0,)), ((), ()))
    back = lax.dot_general(w3[...], error, leading, preferred_element_type=F32)
    delta_2 = (back * slope_of(linear_2, sigmoid_2)).astype(jnp.bfloat16)
    back = lax.dot_general(w2[...], delta_2, leading, preferred_element_type=F32)
    delta_1 = (back * slope_of(linear_1, sigmoid_1)).astype(jnp.bfloat16)
    grad_1 = lax.dot_general(delta_1, inputs, contract, preferred_element_type=F32)
    grad_2 = lax.dot_general(delta_2, hidden_1, contract, preferred_element_type=F32)
    grad_3 = lax.dot_general(hidden_2, error, contract, preferred_element_type=F32)
    outputs = grad_3.shape[1]
    row = lax.broadcasted_iota(jnp.int32, (outputs, 128), 0)
    lane = lax.broadcasted_iota(jnp.int32, (outputs, 128), 1)
    grad_3 = jnp.dot(
        grad_3, jnp.where(lane == row + THIRD_AT, 1.0, 0.0), precision=EXACT, preferred_element_type=F32
    )
    parts = (grad_1[:, :128], grad_1[:, 128:], grad_2[:, :128], grad_2[:, 128:])
    for i, part in enumerate(parts):
        rows = slice(256 * i, 256 * i + 256)
        layers[rows, :] = part if first else layers_in[rows, :] + part
    third[...] = grad_3 if first else third_in[...] + grad_3


def split_kernel(table, layers, third, mine, other):
    first = table[0:1, :] > 0.5
    for ref, at, rows in ((layers, 0, 512), (third, 512, 128)):
        low, high = ref[0:rows, :], ref[rows : 2 * rows, :]
        mine[at : at + rows, :] = jnp.where(first, low, high)
        other[at : at + rows, :] = jnp.where(first, high, low)


def pack_kernel(row, row_other, mine, other, slots):
    upper = lax.broadcasted_iota(jnp.int32, (8, 128), 0) < 4
    inner = row[...] + row_other[...]
    for i in range(slots.shape[0] // 16):
        rows = slice(8 * i, 8 * i + 8)
        tile = mine[rows, :] + other[rows, :]
        for j in range(2):
            at = slice(512 + 2 * i + j, 512 + 2 * i + j + 1)
            below = inner + (mine[at, :] + other[at, :])
            slots[16 * i + 8 * j : 16 * i + 8 * j + 8, :] = jnp.where(upper, pltpu.roll(tile, 4, 0) if j else tile, below)


def pack_again_kernel(row, row_other, share, slots):
    upper = lax.broadcasted_iota(jnp.int32, (8, 128), 0) < 4
    lane = lax.broadcasted_iota(jnp.int32, (8, 128), 1)
    tile = jnp.where(upper | (lane >= THIRD_AT), share[...], row[...] + row_other[...])
    for i in range(slots.shape[0] // 8):
        slots[8 * i : 8 * i + 8, :] = tile


def normal_kernel(table, mine, other, first, second, third, rows, columns):
    low = table[0:1, :] > 0.5
    upper = lax.broadcasted_iota(jnp.int32, (8, 128), 0) < 4
    for i in range(64):
        tiles = []
        for ref in (mine, other):
            tiles.append(
                jnp.where(upper, ref[16 * i : 16 * i + 8, :], pltpu.roll(ref[16 * i + 8 : 16 * i + 16, :], 4, 0))
            )
        rows[8 * i : 8 * i + 8, :] = jnp.where(low, tiles[0], tiles[1])
        rows[512 + 8 * i : 512 + 8 * i + 8, :] = jnp.where(low, tiles[1], tiles[0])
    for at, out in ((0, first), (512, second)):
        part = rows[at : at + 512, :]
        square = jnp.sum(jnp.sum(part * part, axis=0, keepdims=True), axis=1, keepdims=True)
        scale = lax.rsqrt(square / (out.shape[0] * out.shape[1]) + epsilon)
        out[:, :128] = part[:256] * scale
        out[:, 128:] = part[256:] * scale
    own, its = mine[pl.ds(4, 128, stride=8), :], other[pl.ds(4, 128, stride=8), :]
    columns[0:128, :] = jnp.where(low, own, its)
    columns[128:256, :] = jnp.where(low, its, own)
    outputs, channels = third.shape
    row = lax.broadcasted_iota(jnp.int32, (8, 128), 0)
    lane = lax.broadcasted_iota(jnp.int32, (8, 128), 1)
    taken = lax.dot_general(
        jnp.where((lane == row + THIRD_AT) & (row < outputs), 1.0, 0.0), columns[...],
        (((1,), (1,)), ((), ())), precision=EXACT, preferred_element_type=F32,
    )
    square = jnp.sum(jnp.sum(taken * taken, axis=0, keepdims=True), axis=1, keepdims=True)
    taken = taken * lax.rsqrt(square / (outputs * channels) + epsilon)
    third[...] = taken[:outputs]


def body(
    right_side,
    diagonal,
    element_features,
    sample_bank,
    target_bank,
    patch_index,
    w_first,
    w_second,
    w_third,
):
    devices = lax.axis_size(GX_GZ_GA)
    table = tables()
    count = patch_index.shape[0] // GROUPS
    layer_weights = (w_first, w_second, w_third)

    def learn(number, held, waits):
        return call(
            functools.partial(learn_kernel, number, count), ((1024, 128), (256, 128)), (),
            patch_index.reshape(1, -1), sample_bank, target_bank, *layer_weights, *held,
            room=24, aliases={} if number == 0 else {6: 0, 7: 1}, waits=waits, token=True,
        )

    residual, precond, inverse, vector, *faces, token = call(
        start_kernel, (GRID,) * 4 + FACES, (), table, right_side, diagonal, element_features, *layer_weights,
        token=True,
    )
    pressure = share = None
    weights, old_basis, old_images = None, [], []
    gradient = ()
    slots = (8 * devices // 2, 128)
    for number, size in enumerate(BLOCKS):
        final = number + 1 == len(BLOCKS)
        old = len(old_basis)
        basis, images = [vector], []
        for j in range(size - 1):
            halo = exchange(faces)
            waits = ()
            if number == 0 and j < GROUPS:
                *gradient, done = learn(j, gradient, (token,))
                waits = (done,)
            told = number == 0 and j + 1 < GROUPS
            image, vector, *faces = call(
                functools.partial(step_kernel, j == 0), (GRID, GRID) + FACES, HALO_SCRATCH,
                table, basis[-1], basis[max(j - 1, 0)], precond, inverse, *halo, waits=waits, token=told,
            )
            if told:
                token = faces.pop()
            if number == 0 and j == GROUPS - 1:
                mine, other = call(split_kernel, ((640, 128),) * 2, (), table, *gradient)
                other = other_core(other)
            basis.append(vector)
            images.append(image)
        halo = exchange(faces)
        image, row = call(
            functools.partial(last_kernel, size, old), (GRID, (8, 128)), HALO_SCRATCH + ((128, 128),),
            table, precond, residual, *halo, *basis, *images, *old_basis,
        )
        images.append(image)
        if number == 0:
            packed = call(pack_kernel, (slots,), (), row, other_core(row), mine, other)[0]
        else:
            packed = call(pack_again_kernel, (slots,), (), row, other_core(row), share)[0]
        gathered = all_slots(packed)
        given = [gathered, table, residual, *basis, *images]
        shapes = [GRID, GRID]
        if old:
            given += [pressure, weights, *old_basis, *old_images]
        if not final:
            given += [inverse]
            shapes += [GRID, *FACES, (64, 128), (8, 128)]
            if old:
                shapes += [GRID] * (2 * size)
        pressure, residual, *more = call(
            functools.partial(update_kernel, size, old, final), shapes, ((128, 128),), *given
        )
        if not final:
            vector, faces, weights, share = more[0], more[1:7], more[7], more[8]
            old_basis, old_images = basis, images
            if old:
                old_basis, old_images = more[9 : 9 + size], more[9 + size :]
    step_first, step_second, step_third = call(
        normal_kernel, (w_first.shape, w_second.shape, w_third.shape), ((1024, 128), (256, 128)),
        table, gathered, other_core(gathered),
    )
    return (pressure, residual, step_first, step_second, step_third)


def solution(mesh):
    finer = Mesh(
        mesh.devices.reshape(4, 2, 2, mesh.shape["gz"], mesh.shape["ga"]),
        GX_GZ_GA,
    )
    return jax.shard_map(
        body,
        mesh=finer,
        in_specs=(
            P(GX, "ga", "gz"),
            P(GX, "ga", "gz"),
            P(None, GX_GZ_GA),
            P(None, GX_GZ_GA),
            P(None, GX_GZ_GA),
            P(GX_GZ_GA),
            P(),
            P(),
            P(),
        ),
        out_specs=(P(GX, "ga", "gz"), P(GX, "ga", "gz"), P(), P(), P()),
        check_vma=False,
    )
```

```python
import functools

import jax
import jax.numpy as jnp
from jax import lax
from jax.experimental import pallas as pl
from jax.experimental.pallas import tpu as pltpu
from jax.sharding import Mesh
from jax.sharding import PartitionSpec as P

EL = 8
BLOCKS = (6, 6)
GROUPS = 4
GX = ("gx_0", "gx_1", "gx_2")
GX_GZ_GA = ("gx_0", "gx_1", "gx_2", "gz", "ga")
SAME_CORE = ("gx_0", "gx_1", "gz", "ga")

taps = (1.6, -0.2, 8.0 / 315.0, -1.0 / 560.0)
center = 3.0 * 205.0 / 72.0
epsilon = 1e-06
MIDDLE = 1.075
HALF = 0.925
THIRD_AT = 112
EXACT = lax.Precision.HIGHEST
F32 = jnp.float32
VMEM = pl.BlockSpec(memory_space=pltpu.VMEM)
TOKEN = (8, 128)


def after(kernel, count, waits, token, *refs):
    given = refs[:count] + refs[count + waits :]
    if token:
        refs[token][...] = jnp.zeros(TOKEN, F32)
        given = refs[:count] + refs[count + waits : token] + refs[token + 1 :]
    kernel(*given)


def call(kernel, out_shapes, scratch, *args, room=14, aliases={}, waits=(), token=False):
    scratch = [pltpu.VMEM(s, F32) for s in scratch]
    count = len(args)
    args = (*args, *waits)
    out_shapes = (*out_shapes, TOKEN) if token else out_shapes
    kernel = functools.partial(after, kernel, count, len(waits), token and len(args) + len(out_shapes) - 1)
    return pl.pallas_call(
        kernel,
        out_shape=[jax.ShapeDtypeStruct(s, F32) for s in out_shapes],
        in_specs=[VMEM] * len(args),
        out_specs=[VMEM] * len(out_shapes),
        scratch_shapes=scratch,
        input_output_aliases=aliases,
        compiler_params=pltpu.CompilerParams(vmem_limit_bytes=room * 1024 * 1024),
    )(*args)


def pairs(count, odd):
    found = []
    for a in range(odd, count, 2):
        b = (a + 1) % count
        found += [(a, b), (b, a)]
    return found


def exchange(faces):
    xa, xb, ya, yb, za, zb = faces
    nx, ny, nz = lax.axis_size(GX), lax.axis_size("ga"), lax.axis_size("gz")
    return (
        lax.ppermute(xa, GX, pairs(nx, 0)),
        lax.ppermute(xb, GX, pairs(nx, 1)),
        lax.ppermute(ya, "ga", pairs(ny, 0)),
        lax.ppermute(yb, "ga", pairs(ny, 1)),
        lax.ppermute(za, "gz", pairs(nz, 0)),
        lax.ppermute(zb, "gz", pairs(nz, 1)),
    )


def tap_of(distance):
    distance = jnp.abs(distance)
    value = jnp.zeros(distance.shape, F32)
    for offset in range(1, 5):
        value = jnp.where(distance == offset, F32(taps[offset - 1]), value)
    return value


FLAGS, SELECT, SPREAD, BAND = 0, 8, 24, 40


def tables():
    rows = []
    even = {}
    inner = {}
    for name, axis in (("x", GX), ("y", "ga"), ("z", "gz")):
        index, count = lax.axis_index(axis), lax.axis_size(axis)
        even[name] = index % 2 == 0
        inner[name] = (index != 0) & (index != count - 1)
        rows += [even[name], inner[name]]
    rows += [even["x"], even["x"]]
    flags = jnp.broadcast_to(jnp.stack(rows).astype(F32)[:, None], (8, 128))
    row = lax.broadcasted_iota(jnp.int32, (16, 128), 0)
    lane = lax.broadcasted_iota(jnp.int32, (16, 128), 1)
    inside = row % 8
    upper = (row < 8) == even["z"]
    used = inside < 4
    select = jnp.where(used & (lane == inside + jnp.where(upper, 124, 0)), 1.0, 0.0)
    place = inside + jnp.where(upper, 128, -4)
    allowed = used & ((row < 8) | inner["z"])
    spread = jnp.where(allowed, tap_of(lane - place), 0.0)
    out = lax.broadcasted_iota(jnp.int32, (128, 128), 0)
    within = lax.broadcasted_iota(jnp.int32, (128, 128), 1)
    return jnp.concatenate([flags, select, spread, tap_of(out - within)], axis=0)


FACES = ((4, 32, 128), (4, 32, 128), (16, 4, 128), (16, 4, 128), (8, 512), (8, 512))
GRID = (16, 32, 128)


def write_faces(table, field, faces):
    xa, xb, ya, yb, za, zb = faces
    even_x = table[0:1, :] > 0.5
    even_y = table[2:3, :] > 0.5
    xa[...] = jnp.where(even_x, field[12:16], field[0:4])
    xb[...] = jnp.where(even_x, field[0:4], field[12:16])
    ya[...] = jnp.where(even_y, field[:, 28:32, :], field[:, 0:4, :])
    yb[...] = jnp.where(even_y, field[:, 0:4, :], field[:, 28:32, :])
    flat = field[...].reshape(512, 128)
    both = lax.dot_general(
        table[SELECT : SELECT + 16, :], flat, (((1,), (1,)), ((), ())),
        precision=EXACT, preferred_element_type=F32,
    )
    za[...] = both[0:8]
    zb[...] = both[8:16]


def image_planes(table, field, halo, xs, ys, zs, use):
    xa, xb, ya, yb, za, zb = halo
    even_x = table[0:1, :] > 0.5
    keep_x = table[1:2, :] > 0.5
    even_y = table[2:3, :] > 0.5
    keep_y = table[3:4, :] > 0.5
    outer = jnp.where(keep_x, xb[...], 0.0)
    xs[0:4] = jnp.where(even_x, outer, xa[...])
    xs[4:8] = jnp.where(even_x, xa[...], outer)
    outer = jnp.where(keep_y, yb[...], 0.0)
    ys[:, 4:8, :] = jnp.where(even_y, outer, ya[...])
    ys[:, 40:44, :] = jnp.where(even_y, ya[...], outer)
    ys[:, 8:40, :] = field[...]
    flat = field[...].reshape(512, 128)
    arrived = jnp.concatenate([za[...], zb[...]], axis=0)
    zs[...] = jnp.dot(
        flat, table[BAND : BAND + 128, :], precision=EXACT, preferred_element_type=F32
    ) + lax.dot_general(
        arrived, table[SPREAD : SPREAD + 16, :], (((0,), (0,)), ((), ())),
        precision=EXACT, preferred_element_type=F32,
    )

    def plane(i):
        if i < 0:
            return xs[i + 4]
        if i >= 16:
            return xs[i - 12]
        return field[i]

    for i in range(16):
        total = zs[32 * i : 32 * i + 32, :]
        for k in range(1, 5):
            along = (plane(i + k) + plane(i - k)) + (
                ys[i, 8 + k : 40 + k, :] + ys[i, 8 - k : 40 - k, :]
            )
            total = total + taps[k - 1] * along
        use(i, total)


HALO_SCRATCH = ((8, 32, 128), (16, 48, 128), (512, 128))


def start_kernel(table, right, diag, feats, w1, w2, w3, *rest):
    source, precond, inverse, basis = rest[:4]
    faces = rest[4:10]
    hidden = jnp.dot(w1[...], feats[...], preferred_element_type=F32)
    hidden = jax.nn.silu(hidden).astype(jnp.bfloat16)
    hidden = jnp.dot(w2[...], hidden, preferred_element_type=F32)
    hidden = jax.nn.silu(hidden).astype(jnp.bfloat16)
    stress = jnp.dot(w3[...], hidden, preferred_element_type=F32)
    trace = (stress[0:1] + stress[1:2] + stress[2:3]) / 3.0
    row = lax.broadcasted_iota(jnp.int32, (8, 128), 0)
    lane = lax.broadcasted_iota(jnp.int32, (8, 128), 1)
    apart = jnp.where(lane // 16 == row, trace, 0.0)
    element = lax.broadcasted_iota(jnp.int32, (128, 128), 0)
    node = lax.broadcasted_iota(jnp.int32, (128, 128), 1)
    widen = jnp.where(element % 16 == node // EL, 1.0, 0.0)
    wide = jnp.dot(apart, widen, precision=EXACT, preferred_element_type=F32)
    for i in range(16):
        for j in range(4):
            at = (i // EL) * 4 + j
            rows = slice(EL * j, EL * j + EL)
            value = right[i, rows, :] + wide[at : at + 1, :]
            weight = diag[i, rows, :] + center
            source[i, rows, :] = value
            precond[i, rows, :] = weight
            inverted = 1.0 / weight
            inverse[i, rows, :] = inverted
            basis[i, rows, :] = value * inverted
    write_faces(table, basis, faces)


def step_kernel(first, table, field, before, precond, inverse, *rest):
    halo, rest = rest[:6], rest[6:]
    image, after = rest[:2]
    faces, scratch = rest[2:8], rest[8:]

    def use(i, total):
        value = field[i]
        image[i] = precond[i] * value - total
        if first:
            after[i] = ((1.0 - MIDDLE) * value - total * inverse[i]) * (1.0 / HALF)
        else:
            after[i] = ((1.0 - MIDDLE) * value - total * inverse[i]) * (2.0 / HALF) - before[i]

    image_planes(table, field, halo, *scratch, use)
    write_faces(table, after, faces)


def products(size, old):
    wanted = [(("t", i), ("q", j)) for i in range(size) for j in range(i, size)]
    wanted += [(("t", i), ("r", 0)) for i in range(size)]
    groups = [wanted]
    if old:
        for i0 in range(0, old, 4):
            some = range(i0, min(old, i0 + 4))
            groups.append([(("p", i), ("q", j)) for i in some for j in range(size)] + [(("p", i), ("r", 0)) for i in some])
    return groups


def last_kernel(size, old, table, precond, residual, *rest):
    halo, rest = rest[:6], rest[6:]
    basis, rest = rest[:size], rest[size:]
    images, rest = rest[: size - 1], rest[size - 1 :]
    olds, rest = rest[:old], rest[old:]
    image, row = rest[:2]
    scratch, sums = rest[2:5], rest[5]
    field = basis[-1]

    def use(i, total):
        image[i] = precond[i] * field[i] - total

    image_planes(table, field, halo, *scratch, use)
    refs = {("r", 0): residual}
    for j in range(size):
        refs["t", j] = basis[j]
        refs["q", j] = images[j] if j < size - 1 else image
    for j in range(old):
        refs["p", j] = olds[j]
    sums[...] = jnp.zeros(sums.shape, F32)
    at = 0
    for group in products(size, old):
        names = sorted({name for pair in group for name in pair})

        def add(i, totals, names=names, group=group):
            for part in range(4):
                value = {n: refs[n][i, 8 * part : 8 * part + 8, :] for n in names}
                totals = tuple(
                    total + value[a] * value[b] for total, (a, b) in zip(totals, group)
                )
            return totals

        totals = lax.fori_loop(0, 16, add, (jnp.zeros((8, 128), F32),) * len(group))
        for total in totals:
            sums[at : at + 1, :] = jnp.sum(total, axis=0, keepdims=True)
            at += 1
    row[...] = lax.dot_general(
        jnp.ones((8, 128), F32), sums[...], (((1,), (1,)), ((), ())),
        precision=EXACT, preferred_element_type=F32,
    )


def factor(matrix, size):
    low, scaled, inverse = {}, {}, []
    for j in range(size):
        pivot = matrix[j][j]
        for k in range(j):
            pivot = pivot - low[j, k] * scaled[j, k]
        inverse.append(1.0 / pivot)
        for i in range(j + 1, size):
            value = matrix[i][j]
            for k in range(j):
                value = value - scaled[i, k] * low[j, k]
            scaled[i, j] = value
            low[i, j] = value * inverse[j]
    return low, inverse


def solve(factors, size, right):
    low, inverse = factors
    found = []
    for i in range(size):
        value = right[i]
        for k in range(i):
            value = value - low[i, k] * found[k]
        found.append(value)
    found = [a * b for a, b in zip(found, inverse)]
    for i in reversed(range(size)):
        for k in range(i + 1, size):
            found[i] = found[i] - low[k, i] * found[k]
    return found


def update_kernel(size, old, final, *rest):
    gathered, table, residual, rest = rest[0], rest[1], rest[2], rest[3:]
    basis, rest = rest[:size], rest[size:]
    images, rest = rest[:size], rest[size:]
    if old:
        pressure, weights, rest = rest[0], rest[1], rest[2:]
        old_basis, rest = rest[:old], rest[old:]
        old_images, rest = rest[:old], rest[old:]
    if not final:
        inverse, rest = rest[0], rest[1:]
    new_pressure, new_residual = rest[:2]
    rest = rest[2:]
    if not final:
        after, faces, new_weights, share, rest = rest[0], rest[1:7], rest[7], rest[8], rest[9:]
        if old:
            new_basis, rest = rest[:size], rest[size:]
            new_images, rest = rest[:size], rest[size:]
    splats = rest[0]
    total = gathered[0:8, :]
    for i in range(1, gathered.shape[0] // 8):
        total = total + gathered[8 * i : 8 * i + 8, :]
    totals = total[4:5, :]
    row = lax.broadcasted_iota(jnp.int32, (128, 128), 0)
    lane = lax.broadcasted_iota(jnp.int32, (128, 128), 1)
    splats[...] = jnp.dot(
        jnp.where((row == lane) & (lane < THIRD_AT), totals, 0.0), jnp.ones((128, 128), F32),
        precision=EXACT, preferred_element_type=F32,
    )
    if not final:
        share[...] = total
    value = {}
    at = 0
    for group in products(size, old):
        for a, b in group:
            value[a, b] = splats[at : at + 1, :]
            at += 1
    gram = [[value[("t", min(i, j)), ("q", max(i, j))] for j in range(size)] for i in range(size)]
    right = [value[("t", i), ("r", 0)] for i in range(size)]
    mix = None
    if old:
        cross = [[value[("p", i), ("q", j)] for j in range(size)] for i in range(old)]
        held = [[weights[i * old + j : i * old + j + 1, :] for j in range(old)] for i in range(old)]
        factors = factor(held, old)
        columns = [solve(factors, old, [-cross[i][j] for i in range(old)]) for j in range(size)]
        behind = [value[("p", i), ("r", 0)] for i in range(old)]
        for j in range(size):
            for k in range(old):
                right[j] = right[j] + columns[j][k] * behind[k]
        behind = solve(factors, old, behind)
        for i in range(size):
            for j in range(i, size):
                for k in range(old):
                    gram[i][j] = gram[i][j] + cross[k][i] * columns[j][k]
                gram[j][i] = gram[i][j]
        mix = [[jnp.broadcast_to(v, (8, 128)) for v in column] for column in columns]
    step = solve(factor(gram, size), size, right)
    if not final:
        new_weights[...] = jnp.zeros(new_weights.shape, F32)
        for i in range(size):
            for j in range(size):
                new_weights[i * size + j : i * size + j + 1, :] = gram[i][j]
    if old:
        carried = []
        for i in range(old):
            total = behind[i]
            if final:
                for j in range(size):
                    total = total + step[j] * columns[j][i]
            carried.append(jnp.broadcast_to(total, (8, 128)))
    step = [jnp.broadcast_to(v, (8, 128)) for v in step]

    def tile(i, part):
        rows = slice(8 * part, 8 * part + 8)
        vectors = [ref[i, rows, :] for ref in basis]
        duals = [ref[i, rows, :] for ref in images]
        if old and not final:
            held_v = [ref[i, rows, :] for ref in old_basis]
            held_d = [ref[i, rows, :] for ref in old_images]
            for j in range(size):
                for k in range(old):
                    vectors[j] = vectors[j] + mix[j][k] * held_v[k]
                    duals[j] = duals[j] + mix[j][k] * held_d[k]
                new_basis[j][i, rows, :] = vectors[j]
                new_images[j][i, rows, :] = duals[j]
        gain = step[0] * vectors[0]
        loss = step[0] * duals[0]
        for j in range(1, size):
            gain = gain + step[j] * vectors[j]
            loss = loss + step[j] * duals[j]
        if old:
            for k in range(old):
                gain = gain + carried[k] * old_basis[k][i, rows, :]
                loss = loss + carried[k] * old_images[k][i, rows, :]
        if old:
            gain = pressure[i, rows, :] + gain
        left = residual[i, rows, :] - loss
        new_pressure[i, rows, :] = gain
        new_residual[i, rows, :] = left
        if not final:
            after[i, rows, :] = left * inverse[i, rows, :]

    def planes(i, nothing):
        for part in range(4):
            tile(i, part)
        return nothing

    lax.fori_loop(0, 16, planes, 0)
    if not final:
        write_faces(table, after, faces)


def all_slots(slots):
    return lax.all_to_all(slots, SAME_CORE, split_axis=0, concat_axis=0, tiled=True)


def other_core(array):
    return lax.ppermute(array, GX[-1], pairs(2, 0))


def slope_of(linear, sigmoid):
    return sigmoid * (1.0 + linear * (1.0 - sigmoid))


def learn_kernel(number, group, index, bank, target, w1, w2, w3, *rest):
    first = number == 0
    if not first:
        layers_in, third_in, rest = rest[0], rest[1], rest[2:]
    layers, third = rest
    column = lax.broadcasted_iota(jnp.int32, (bank.shape[1], group), 0)
    chosen = jnp.where(column == index[:, group * number : group * number + group], 1.0, 0.0).astype(jnp.bfloat16)
    inputs = jnp.dot(bank[...], chosen, preferred_element_type=F32).astype(jnp.bfloat16)
    wanted = jnp.dot(target[...], chosen, preferred_element_type=F32)
    linear_1 = jnp.dot(w1[...], inputs, preferred_element_type=F32)
    sigmoid_1 = 1.0 / (1.0 + jnp.exp(-linear_1))
    hidden_1 = (linear_1 * sigmoid_1).astype(jnp.bfloat16)
    linear_2 = jnp.dot(w2[...], hidden_1, preferred_element_type=F32)
    sigmoid_2 = 1.0 / (1.0 + jnp.exp(-linear_2))
    hidden_2 = (linear_2 * sigmoid_2).astype(jnp.bfloat16)
    stress = jnp.dot(w3[...], hidden_2, preferred_element_type=F32)
    error = (stress - wanted).astype(jnp.bfloat16)
    contract = (((1,), (1,)), ((), ()))
    leading = (((0,), (0,)), ((), ()))
    back = lax.dot_general(w3[...], error, leading, preferred_element_type=F32)
    delta_2 = (back * slope_of(linear_2, sigmoid_2)).astype(jnp.bfloat16)
    back = lax.dot_general(w2[...], delta_2, leading, preferred_element_type=F32)
    delta_1 = (back * slope_of(linear_1, sigmoid_1)).astype(jnp.bfloat16)
    grad_1 = lax.dot_general(delta_1, inputs, contract, preferred_element_type=F32)
    grad_2 = lax.dot_general(delta_2, hidden_1, contract, preferred_element_type=F32)
    grad_3 = lax.dot_general(hidden_2, error, contract, preferred_element_type=F32)
    outputs = grad_3.shape[1]
    row = lax.broadcasted_iota(jnp.int32, (outputs, 128), 0)
    lane = lax.broadcasted_iota(jnp.int32, (outputs, 128), 1)
    grad_3 = jnp.dot(
        grad_3, jnp.where(lane == row + THIRD_AT, 1.0, 0.0), precision=EXACT, preferred_element_type=F32
    )
    parts = (grad_1[:, :128], grad_1[:, 128:], grad_2[:, :128], grad_2[:, 128:])
    for i, part in enumerate(parts):
        rows = slice(256 * i, 256 * i + 256)
        layers[rows, :] = part if first else layers_in[rows, :] + part
    third[...] = grad_3 if first else third_in[...] + grad_3


def split_kernel(table, layers, third, mine, other):
    first = table[0:1, :] > 0.5
    for ref, at, rows in ((layers, 0, 512), (third, 512, 128)):
        low, high = ref[0:rows, :], ref[rows : 2 * rows, :]
        mine[at : at + rows, :] = jnp.where(first, low, high)
        other[at : at + rows, :] = jnp.where(first, high, low)


def pack_kernel(row, row_other, mine, other, slots):
    upper = lax.broadcasted_iota(jnp.int32, (8, 128), 0) < 4
    inner = row[...] + row_other[...]
    for i in range(slots.shape[0] // 16):
        rows = slice(8 * i, 8 * i + 8)
        tile = mine[rows, :] + other[rows, :]
        for j in range(2):
            at = slice(512 + 2 * i + j, 512 + 2 * i + j + 1)
            below = inner + (mine[at, :] + other[at, :])
            slots[16 * i + 8 * j : 16 * i + 8 * j + 8, :] = jnp.where(upper, pltpu.roll(tile, 4, 0) if j else tile, below)


def pack_again_kernel(row, row_other, share, slots):
    upper = lax.broadcasted_iota(jnp.int32, (8, 128), 0) < 4
    lane = lax.broadcasted_iota(jnp.int32, (8, 128), 1)
    tile = jnp.where(upper | (lane >= THIRD_AT), share[...], row[...] + row_other[...])
    for i in range(slots.shape[0] // 8):
        slots[8 * i : 8 * i + 8, :] = tile


def normal_kernel(table, mine, other, first, second, third, rows, columns):
    low = table[0:1, :] > 0.5
    upper = lax.broadcasted_iota(jnp.int32, (8, 128), 0) < 4
    for i in range(64):
        tiles = []
        for ref in (mine, other):
            tiles.append(
                jnp.where(upper, ref[16 * i : 16 * i + 8, :], pltpu.roll(ref[16 * i + 8 : 16 * i + 16, :], 4, 0))
            )
        rows[8 * i : 8 * i + 8, :] = jnp.where(low, tiles[0], tiles[1])
        rows[512 + 8 * i : 512 + 8 * i + 8, :] = jnp.where(low, tiles[1], tiles[0])
    for at, out in ((0, first), (512, second)):
        part = rows[at : at + 512, :]
        square = jnp.sum(jnp.sum(part * part, axis=0, keepdims=True), axis=1, keepdims=True)
        scale = lax.rsqrt(square / (out.shape[0] * out.shape[1]) + epsilon)
        out[:, :128] = part[:256] * scale
        out[:, 128:] = part[256:] * scale
    own, its = mine[pl.ds(4, 128, stride=8), :], other[pl.ds(4, 128, stride=8), :]
    columns[0:128, :] = jnp.where(low, own, its)
    columns[128:256, :] = jnp.where(low, its, own)
    outputs, channels = third.shape
    row = lax.broadcasted_iota(jnp.int32, (8, 128), 0)
    lane = lax.broadcasted_iota(jnp.int32, (8, 128), 1)
    taken = lax.dot_general(
        jnp.where((lane == row + THIRD_AT) & (row < outputs), 1.0, 0.0), columns[...],
        (((1,), (1,)), ((), ())), precision=EXACT, preferred_element_type=F32,
    )
    square = jnp.sum(jnp.sum(taken * taken, axis=0, keepdims=True), axis=1, keepdims=True)
    taken = taken * lax.rsqrt(square / (outputs * channels) + epsilon)
    third[...] = taken[:outputs]


def body(
    right_side,
    diagonal,
    element_features,
    sample_bank,
    target_bank,
    patch_index,
    w_first,
    w_second,
    w_third,
):
    devices = lax.axis_size(GX_GZ_GA)
    table = tables()
    count = patch_index.shape[0] // GROUPS
    layer_weights = (w_first, w_second, w_third)

    def learn(number, held, waits):
        return call(
            functools.partial(learn_kernel, number, count), ((1024, 128), (256, 128)), (),
            patch_index.reshape(1, -1), sample_bank, target_bank, *layer_weights, *held,
            room=24, aliases={} if number == 0 else {6: 0, 7: 1}, waits=waits, token=True,
        )

    residual, precond, inverse, vector, *faces = call(
        start_kernel, (GRID,) * 4 + FACES, (), table, right_side, diagonal, element_features, *layer_weights,
    )
    pressure = share = None
    weights, old_basis, old_images = None, [], []
    gradient = ()
    slots = (8 * devices // 2, 128)
    for number, size in enumerate(BLOCKS):
        final = number + 1 == len(BLOCKS)
        old = len(old_basis)
        basis, images = [vector], []
        for j in range(size - 1):
            halo = exchange(faces)
            waits = ()
            if number == 0 and 1 <= j <= GROUPS:
                *gradient, done = learn(j - 1, gradient, (token,))
                waits = (done,)
            told = number == 0 and j < GROUPS
            image, vector, *faces = call(
                functools.partial(step_kernel, j == 0), (GRID, GRID) + FACES, HALO_SCRATCH,
                table, basis[-1], basis[max(j - 1, 0)], precond, inverse, *halo, waits=waits, token=told,
            )
            if told:
                token = faces.pop()
            if number == 0 and j == GROUPS:
                mine, other = call(split_kernel, ((640, 128),) * 2, (), table, *gradient)
                other = other_core(other)
            basis.append(vector)
            images.append(image)
        halo = exchange(faces)
        image, row = call(
            functools.partial(last_kernel, size, old), (GRID, (8, 128)), HALO_SCRATCH + ((128, 128),),
            table, precond, residual, *halo, *basis, *images, *old_basis,
        )
        images.append(image)
        if number == 0:
            packed = call(pack_kernel, (slots,), (), row, other_core(row), mine, other)[0]
        else:
            packed = call(pack_again_kernel, (slots,), (), row, other_core(row), share)[0]
        gathered = all_slots(packed)
        given = [gathered, table, residual, *basis, *images]
        shapes = [GRID, GRID]
        if old:
            given += [pressure, weights, *old_basis, *old_images]
        if not final:
            given += [inverse]
            shapes += [GRID, *FACES, (64, 128), (8, 128)]
            if old:
                shapes += [GRID] * (2 * size)
        pressure, residual, *more = call(
            functools.partial(update_kernel, size, old, final), shapes, ((128, 128),), *given
        )
        if not final:
            vector, faces, weights, share = more[0], more[1:7], more[7], more[8]
            old_basis, old_images = basis, images
            if old:
                old_basis, old_images = more[9 : 9 + size], more[9 + size :]
    step_first, step_second, step_third = call(
        normal_kernel, (w_first.shape, w_second.shape, w_third.shape), ((1024, 128), (256, 128)),
        table, gathered, other_core(gathered),
    )
    return (pressure, residual, step_first, step_second, step_third)


def solution(mesh):
    finer = Mesh(
        mesh.devices.reshape(4, 2, 2, mesh.shape["gz"], mesh.shape["ga"]),
        GX_GZ_GA,
    )
    return jax.shard_map(
        body,
        mesh=finer,
        in_specs=(
            P(GX, "ga", "gz"),
            P(GX, "ga", "gz"),
            P(None, GX_GZ_GA),
            P(None, GX_GZ_GA),
            P(None, GX_GZ_GA),
            P(GX_GZ_GA),
            P(),
            P(),
            P(),
        ),
        out_specs=(P(GX, "ga", "gz"), P(GX, "ga", "gz"), P(), P(), P()),
        check_vma=False,
    )
```
